32 devices in a mesh: parts: 2 (over x), wide: 16 (over z, y, core).
Axes of the slice: x: 2, y: 2, z: 4, core: 2. Of those that a mesh axis runs over, the one named last changes fastest.
Arguments:
- potential_pool: bfloat16 [32, 512, 512], P(('parts', 'wide')), parts along dimension 0, may hold values from 0 to 1.5
- slice_owner: int32 [4], P('parts'), parts along dimension 0, may hold values from 0 to 15
- beam_index: int32 [16, 2], replicated, may hold values from -128 to 127
- aperture: int32 [16], replicated, may hold values 0 or 1
- probe_position: int32 [16, 2], P('parts'), parts along dimension 0, may hold values from 0 to 511
Outputs:
- probes: float32 [512, 2, 8, 256], P(('parts', 'wide')), parts along dimension 0
The draws below stay inside these ranges and needn't reach their ends.
There are 2 independent parts, one for each index of `parts`. The reference program is written for one: setup_inputs(seed, part) draws one part's arguments, and reference() takes and returns one part's arrays. A program takes and returns all parts, laid end to end along the dimension named above; an argument that names none is the same for every part. Nothing has to cross between parts.
All inputs are finite; a program needn't handle non-finite values.
Results may differ from the reference program's by a relative error of at most 0.0003.
Values may be sent and summed in bfloat16 or wider, within the bound.
No kernel may reach another device: no remote copies, remote signals or barrier semaphores. Data moves between devices by JAX's collectives and lax.ppermute only.
A program may use at most 64 MiB of HBM per device.

```python
import math
import jax
import jax.numpy as jnp
from jax import lax

GRID = 512
PROBES = 8
SLICES = 2
BEAMS = 16
SLABS = 16


def set_ends(drawn, own_key, smallest, high):
    shape = drawn.shape
    index_at = [jax.random.randint(jax.random.fold_in(own_key, axis), (), 0, shape[axis]) for axis in range(len(shape))]
    drawn = drawn.at[tuple(index_at)].set(smallest)
    longest = shape.index(max(shape))
    index_at[longest] = (index_at[longest] + 1) % shape[longest]
    return drawn.at[tuple(index_at)].set(high)


def block_levels(rng, shape, shards, low, top_value):
    level = 1.0
    for axis_at, blocks in shards:
        heights = jax.random.uniform(jax.random.fold_in(jax.random.fold_in(rng, 6), axis_at), (blocks,), jnp.float32, low / len(shards), top_value / len(shards))
        level = level * jnp.repeat(jnp.exp(heights), shape[axis_at] // blocks).reshape((-1,) + (1,) * (len(shape) - 1 - axis_at))
    return level


def setup_inputs(seed: int = 0, part: int = 0) -> dict:
    splits = jax.random.split(jax.random.key(seed), 6)
    part_keys = jax.random.split(jax.random.fold_in(splits[5], part), 6)
    return {
        "potential_pool": jnp.clip(1.5 * jax.random.uniform(part_keys[0], (SLABS, GRID, GRID), jnp.float32) ** block_levels(part_keys[0], (SLABS, GRID, GRID), ((0, 16),), -0.2, 0.2), 0.0, 1.5).astype(jnp.bfloat16),
        "slice_owner": jax.random.randint(part_keys[1], (SLICES,), 0, SLABS).astype(jnp.int32),
        "beam_index": set_ends(jax.random.randint(splits[2], (BEAMS, 2), -(GRID // 4), GRID // 4), jax.random.fold_in(splits[2], 1), -(GRID // 4), (GRID // 4) - 1).astype(jnp.int32),
        "aperture": set_ends((jax.random.randint(splits[3], (BEAMS,), 0, 4) < 3).astype(jnp.int32), jax.random.fold_in(splits[3], 1), 0, 1),
        "probe_position": set_ends(jax.random.randint(part_keys[4], (PROBES, 2), 0, GRID), jax.random.fold_in(part_keys[4], 1), 0, GRID - 1).astype(jnp.int32),
    }


FRESNEL = 4.7e-05

def reference(potential_pool, slice_owner, beam_index, aperture, probe_position):
    grid = potential_pool.shape[-1]
    crop = grid // 2
    margin = grid // 4
    pixels = jnp.arange(grid, dtype=jnp.int32)
    centred = jnp.mod(pixels + grid // 2, grid) - grid // 2
    squared = centred[:, None] * centred[:, None] + centred[None, :] * centred[None, :]
    keep = (9 * squared <= grid * grid).astype(jnp.float32)
    turning = -FRESNEL * squared.astype(jnp.float32)
    propagator = jnp.cos(turning) * keep + 1j * (jnp.sin(turning) * keep)
    transmit = []
    for slab_number in range(SLICES):
        phase = potential_pool[slice_owner[slab_number]].astype(jnp.float32)
        transmit.append(jnp.cos(phase) + 1j * jnp.sin(phase))
    mixing = jnp.mod(beam_index[:, 0][None, :] * probe_position[:, 0][:, None] + beam_index[:, 1][None, :] * probe_position[:, 1][:, None], grid)
    coef_angle = -2.0 * math.pi * mixing.astype(jnp.float32) / grid
    weight = aperture.astype(jnp.float32) / math.sqrt(BEAMS)
    coef_real = jnp.cos(coef_angle) * weight[None, :]
    coef_imag = jnp.sin(coef_angle) * weight[None, :]

    def one_beam(total, inputs):
        freq, col_real, col_imag = inputs
        turns = jnp.mod(freq[0] * pixels[:, None] + freq[1] * pixels[None, :], grid)
        angle = 2.0 * math.pi * turns.astype(jnp.float32) / grid
        wave = jnp.cos(angle) + 1j * jnp.sin(angle)
        for slab_number in range(SLICES):
            wave = wave * transmit[slab_number]
            wave = jnp.fft.ifft2(jnp.fft.fft2(wave) * propagator)
        cut = wave[margin:margin + crop, margin:margin + crop]
        cut_real = jnp.real(cut)
        cut_imag = jnp.imag(cut)
        add_real = col_real[None, :, None] * cut_real[:, None, :] - col_imag[None, :, None] * cut_imag[:, None, :]
        add_imag = col_real[None, :, None] * cut_imag[:, None, :] + col_imag[None, :, None] * cut_real[:, None, :]
        return (total + jnp.stack([add_real, add_imag], axis=1), None)
    start = jnp.zeros((crop, 2, probe_position.shape[0], crop), jnp.float32)
    total, unused = lax.scan(one_beam, start, (beam_index, coef_real.T, coef_imag.T))
    return total
```

```python
import math

import jax
import jax.numpy as jnp
import numpy as np
from jax import lax
from jax.experimental import pallas as pl
from jax.experimental.pallas import tpu as pltpu
from jax.sharding import PartitionSpec as P

FRESNEL = 4.7e-05
TWO_PI = 2.0 * math.pi
F32 = jnp.float32
BF16 = jnp.bfloat16
QUAD = 4


def flip(array, bit, groups):
    return lax.ppermute(array, "wide", [(i, i ^ bit) for i in range(groups)])


def half(array, which):
    rows = array.shape[0] // 2
    return lax.dynamic_slice_in_dim(array, which * rows, rows, 0)


def spread_slabs(own_slab, slice_owner, groups, device):
    count = slice_owner.shape[0]
    bits = [1 << b for b in range(groups.bit_length() - 1)]
    side = device & 1
    kept = half(own_slab, side)
    received = flip(half(own_slab, 1 - side), 1, groups)
    zero = jnp.zeros_like(kept)
    parts = [
        jnp.where(slice_owner[s] == device, kept, jnp.where(slice_owner[s] == (device ^ 1), received, zero))
        for s in range(count)
    ]
    for bit in bits[1:-1]:
        side = (device // bit) & 1
        parts = [half(part, side) + flip(half(part, 1 - side), bit, groups) for part in parts]
    parts = [part + flip(part, bits[-1], groups) for part in parts]
    for bit in reversed(bits[:-1]):
        side = (device // bit) & 1
        grown = []
        for part in parts:
            other = flip(part, bit, groups)
            low = jnp.where(side == 0, part, other)
            high = jnp.where(side == 0, other, part)
            grown.append(jnp.concatenate([low, high], axis=0))
        parts = grown
    return parts


def class_frequencies(grid):
    top = grid // 3
    classes = [[u for u in range(-top, top + 1) if u % 4 == c] for c in range(4)]
    padded = -(-max(len(c) for c in classes) // 8) * 8
    freq = np.zeros((4, padded), np.int32)
    real = np.zeros((4, padded), np.float32)
    for c, members in enumerate(classes):
        freq[c, : len(members)] = members
        real[c, : len(members)] = 1.0
    return freq, real


def split_table(table):
    high = lax.reduce_precision(table, 8, 7)
    return high.astype(BF16), (table - high).astype(BF16)


def block(a, b, c, d):
    return jnp.concatenate([jnp.concatenate([a, b], axis=-1), jnp.concatenate([c, d], axis=-1)], axis=-2)


def make_tables(grid):
    freq, real = class_frequencies(grid)
    kp = freq.shape[1]
    q = grid // 4
    turns = np.mod(freq[:, None, :].astype(np.int64) * np.arange(q)[None, :, None], grid)
    angle = TWO_PI * turns / grid
    cos = np.zeros((4, q, q), np.float32)
    sin = np.zeros((4, q, q), np.float32)
    cos[:, :, :kp] = np.cos(angle) * real[:, None, :]
    sin[:, :, :kp] = np.sin(angle) * real[:, None, :]
    cos, sin = lax.optimization_barrier((jnp.asarray(cos), jnp.asarray(sin)))
    cos_t, sin_t = jnp.swapaxes(cos, 1, 2), jnp.swapaxes(sin, 1, 2)
    lane_fwd = block(cos, -sin, sin, cos)
    row_fwd = block(cos_t[:, :kp], sin_t[:, :kp], -sin_t[:, :kp], cos_t[:, :kp])
    row_inv = block(cos[:, :, :kp], -sin[:, :, :kp], sin[:, :, :kp], cos[:, :, :kp])
    lane_inv = block(cos_t, sin_t, -sin_t, cos_t)
    return [split_table(t) for t in (lane_fwd, row_fwd, row_inv, lane_inv)]


def make_propagator(grid):
    freq, real = class_frequencies(grid)
    kp = freq.shape[1]
    q = grid // 4
    lanes = np.full((4, q), grid, np.int32)
    lanes[:, :kp] = np.where(real > 0, freq, grid)
    rows = np.where(real > 0, freq, grid)
    rows, lanes = lax.optimization_barrier((jnp.asarray(rows, jnp.int32), jnp.asarray(lanes.reshape(-1), jnp.int32)))
    squared = (rows * rows)[:, :, None] + (lanes * lanes)[None, None, :]
    keep = (9 * squared <= grid * grid).astype(F32) * (1.0 / (grid * grid))
    turning = -FRESNEL * squared.astype(F32)
    return jnp.cos(turning) * keep, jnp.sin(turning) * keep


def rows_table(grid, first_row, rows):
    freq, real = class_frequencies(grid)
    x = first_row + jnp.arange(rows, dtype=jnp.int32)
    turns = jnp.mod(x[None, :, None] * jnp.asarray(freq)[:, None, :], grid)
    angle = TWO_PI * turns.astype(F32) / grid
    cos = jnp.cos(angle) * jnp.asarray(real)[:, None, :]
    sin = jnp.sin(angle) * jnp.asarray(real)[:, None, :]
    return split_table(block(cos, -sin, sin, cos))


def probe_waves(grid, beam_index, aperture, position):
    beams = beam_index.shape[0]
    pixels = jnp.arange(grid, dtype=jnp.int32)

    def turned(turns, sign):
        angle = sign * TWO_PI * jnp.mod(turns, grid).astype(F32) / grid
        return jnp.cos(angle), jnp.sin(angle)

    weight = aperture.astype(F32) / math.sqrt(beams)
    mixing = beam_index[:, 0][None, :] * position[:, 0][:, None] + beam_index[:, 1][None, :] * position[:, 1][:, None]
    coef_r, coef_i = turned(mixing, -1.0)
    coef_r, coef_i = coef_r * weight[None, :], coef_i * weight[None, :]
    row_r, row_i = turned(pixels[:, None] * beam_index[:, 0][None, :], 1.0)
    col_r, col_i = turned(beam_index[:, 1][:, None] * pixels[None, :], 1.0)
    left_r = coef_r[:, None, :] * row_r - coef_i[:, None, :] * row_i
    left_i = coef_r[:, None, :] * row_i + coef_i[:, None, :] * row_r
    left = jnp.concatenate([left_r, left_i], axis=-1)
    right = jnp.stack([jnp.concatenate([col_r, -col_i], axis=0), jnp.concatenate([col_i, col_r], axis=0)])
    return jnp.einsum("pxb,rby->prxy", left, right, precision=lax.Precision.HIGHEST)


def split(x):
    high = x.astype(BF16)
    return high, (x - high.astype(F32)).astype(BF16)


def dot(a, b):
    return jnp.dot(a, b, preferred_element_type=F32)


def dot3(ah, al, bh, bl):
    return dot(ah, bh) + dot(al, bh) + dot(ah, bl)


def butterfly(parts, sign):
    (r0, i0), (r1, i1), (r2, i2), (r3, i3) = parts
    sr, si, dr, di = r0 + r2, i0 + i2, r0 - r2, i0 - i2
    tr, ti, er, ei = r1 + r3, i1 + i3, r1 - r3, i1 - i3
    up = (dr - sign * ei, di + sign * er)
    down = (dr + sign * ei, di - sign * er)
    return [(sr + tr, si + ti), up, (sr - tr, si - ti), down]


def cos_sin(v):
    t = v * v
    c = 1.0
    for n in range(14, 0, -2):
        c = 1.0 - t * (1.0 / (n * (n - 1))) * c
    s = 1.0
    for n in range(15, 1, -2):
        s = 1.0 - t * (1.0 / (n * (n - 1))) * s
    return c, v * s


def transmit_tables(slab_ref, tr_ref, ti_ref):
    rows = 32
    q = slab_ref.shape[1] // 4

    def body(b, carry):
        at = pl.ds(pl.multiple_of(b * rows, rows), rows)
        for j in range(4):
            lanes = pl.ds(j * q, q)
            c, s = cos_sin(slab_ref[at, lanes].astype(F32))
            tr_ref[at, lanes] = c
            ti_ref[at, lanes] = s
        return carry

    lax.fori_loop(0, slab_ref.shape[0] // rows, body, 0)


def forward(wave_ref, tr_ref, ti_ref, lane, row, prop, scratch):
    yh, yl, sr, si, zh, zl, uh, ul = scratch
    n = tr_ref.shape[0]
    q = n // 4
    kp2 = uh.shape[1]
    kp = kp2 // 2
    rows = 32

    def fold_lanes(b, carry):
        at = pl.ds(pl.multiple_of(b * rows, rows), rows)
        parts = []
        for j in range(4):
            lanes = pl.ds(j * q, q)
            wr, wi = wave_ref[0, 0, at, lanes], wave_ref[0, 1, at, lanes]
            cr, ci = tr_ref[at, lanes], ti_ref[at, lanes]
            parts.append((wr * cr - wi * ci, wr * ci + wi * cr))
        for c, (r, i) in enumerate(butterfly(parts, -1.0)):
            yh[c, at, :q], yl[c, at, :q] = split(r)
            yh[c, at, q:], yl[c, at, q:] = split(i)
        return carry

    lax.fori_loop(0, n // rows, fold_lanes, 0)
    for c in range(4):
        out = dot3(yh[c], yl[c], lane[0][c], lane[1][c])
        sr[:, c * q : (c + 1) * q] = out[:, :q]
        si[:, c * q : (c + 1) * q] = out[:, q:]

    def fold_rows(b, carry):
        first = pl.multiple_of(b * rows, rows)
        for l in range(4):
            lanes = pl.ds(l * q, q)
            parts = [(sr[pl.ds(j * q + first, rows), lanes], si[pl.ds(j * q + first, rows), lanes]) for j in range(4)]
            for c, (r, i) in enumerate(butterfly(parts, -1.0)):
                zh[c, pl.ds(first, rows), lanes], zl[c, pl.ds(first, rows), lanes] = split(r)
                zh[c, pl.ds(q + first, rows), lanes], zl[c, pl.ds(q + first, rows), lanes] = split(i)
        return carry

    lax.fori_loop(0, q // rows, fold_rows, 0)
    for c in range(4):
        out = dot3(row[0][c], row[1][c], zh[c], zl[c])
        r, i = out[:kp], out[kp:]
        pr, pi = prop[0][c], prop[1][c]
        uh[c], ul[c] = split(jnp.concatenate([r * pr - i * pi, r * pi + i * pr], axis=0))


def first_kernel(slab_ref, wave_ref, lfh, lfl, rfh, rfl, rih, ril, lih, lil, pr, pi, out_ref, tr, ti, yh, yl, sr, si, zh, zl, uh, ul, g, h):
    n = slab_ref.shape[0]
    q = n // 4
    rows = 32

    @pl.when(pl.program_id(0) == 0)
    def _():
        transmit_tables(slab_ref, tr, ti)

    forward(wave_ref, tr, ti, (lfh, lfl), (rfh, rfl), (pr, pi), (yh, yl, sr, si, zh, zl, uh, ul))
    for c in range(4):
        g[c] = dot3(rih[c], ril[c], uh[c], ul[c])

    def unfold_rows(b, carry):
        first = pl.multiple_of(b * rows, rows)
        for l in range(4):
            lanes = pl.ds(l * q, q)
            parts = [(g[c, pl.ds(first, rows), lanes], g[c, pl.ds(q + first, rows), lanes]) for c in range(4)]
            for j, (r, i) in enumerate(butterfly(parts, 1.0)):
                yh[l, pl.ds(j * q + first, rows), :q], yl[l, pl.ds(j * q + first, rows), :q] = split(r)
                yh[l, pl.ds(j * q + first, rows), q:], yl[l, pl.ds(j * q + first, rows), q:] = split(i)
        return carry

    lax.fori_loop(0, q // rows, unfold_rows, 0)
    for c in range(4):
        h[c] = dot3(yh[c], yl[c], lih[c], lil[c])

    def unfold_lanes(b, carry):
        at = pl.ds(pl.multiple_of(b * rows, rows), rows)
        parts = [(h[c, at, :q], h[c, at, q:]) for c in range(4)]
        for j, (r, i) in enumerate(butterfly(parts, 1.0)):
            out_ref[0, 0, at, pl.ds(j * q, q)] = r
            out_ref[0, 1, at, pl.ds(j * q, q)] = i
        return carry

    lax.fori_loop(0, n // rows, unfold_lanes, 0)


def last_kernel(slab_ref, wave_ref, lfh, lfl, rfh, rfl, dh, dl, lih, lil, pr, pi, out_ref, tr, ti, yh, yl, sr, si, zh, zl, uh, ul):
    n = slab_ref.shape[0]
    q = n // 4
    take = dh.shape[1] // 2

    @pl.when(pl.program_id(0) == 0)
    def _():
        transmit_tables(slab_ref, tr, ti)

    forward(wave_ref, tr, ti, (lfh, lfl), (rfh, rfl), (pr, pi), (yh, yl, sr, si, zh, zl, uh, ul))
    out = dot3(dh[0], dl[0], uh[0], ul[0])
    for c in range(1, 4):
        out = out + dot3(dh[c], dl[c], uh[c], ul[c])
    parts = []
    for c in range(4):
        lanes = slice(c * q, (c + 1) * q)
        high, low = split(jnp.concatenate([out[:take, lanes], out[take:, lanes]], axis=1))
        back = dot3(high, low, lih[c], lil[c])
        parts.append((back[:, :q], back[:, q:]))
    for j, (r, i) in enumerate(butterfly(parts, 1.0)[1:3]):
        out_ref[0, 0, :, j * q : (j + 1) * q] = r
        out_ref[0, 1, :, j * q : (j + 1) * q] = i


def whole(array):
    return pl.BlockSpec(array.shape, lambda p: (0,) * array.ndim, pipeline_mode=pl.Buffered(1))


def one(shape):
    return pl.BlockSpec((1,) + shape[1:], lambda p: (p,) + (0,) * (len(shape) - 1))


def forward_scratch(n, kp2):
    q = n // 4
    return [
        pltpu.VMEM((n, n), F32),
        pltpu.VMEM((n, n), F32),
        pltpu.VMEM((4, n, 2 * q), BF16),
        pltpu.VMEM((4, n, 2 * q), BF16),
        pltpu.VMEM((n, n), F32),
        pltpu.VMEM((n, n), F32),
        pltpu.VMEM((4, 2 * q, n), BF16),
        pltpu.VMEM((4, 2 * q, n), BF16),
        pltpu.VMEM((4, kp2, n), BF16),
        pltpu.VMEM((4, kp2, n), BF16),
    ]


def run_kernel(kernel, name, slab, waves, tables, out_shape, extra):
    n = slab.shape[0]
    kp2 = tables[2].shape[1]
    return pl.pallas_call(
        kernel,
        name=name,
        grid=(waves.shape[0],),
        in_specs=[whole(slab), one(waves.shape)] + [whole(t) for t in tables],
        out_specs=one(out_shape),
        out_shape=jax.ShapeDtypeStruct(out_shape, F32),
        scratch_shapes=forward_scratch(n, kp2) + extra,
        compiler_params=pltpu.CompilerParams(vmem_limit_bytes=48 << 20),
    )(slab, waves, *tables)


def local(potential_pool, slice_owner, beam_index, aperture, probe_position):
    grid = potential_pool.shape[-1]
    crop = grid // 2
    margin = grid // 4
    q = grid // 4
    groups = lax.axis_size("wide")
    device = lax.axis_index("wide")
    probes = probe_position.shape[0]
    per_device = probes // QUAD
    quad_rows = crop // (groups // QUAD)
    own_rows = crop // groups
    place = device % QUAD
    quad = device // QUAD

    slabs = spread_slabs(potential_pool[0], slice_owner, groups, device)

    position = lax.dynamic_slice_in_dim(probe_position, place * per_device, per_device, 0)
    waves = probe_waves(grid, beam_index, aperture, position)
    lane_fwd, row_fwd, row_inv, lane_inv = make_tables(grid)
    prop = make_propagator(grid)
    last_rows = rows_table(grid, margin + quad * quad_rows, quad_rows)

    for slab in slabs[:-1]:
        tables = (*lane_fwd, *row_fwd, *row_inv, *lane_inv, *prop)
        extra = [pltpu.VMEM((4, 2 * q, grid), F32), pltpu.VMEM((4, grid, 2 * q), F32)]
        waves = run_kernel(first_kernel, "slice_full", slab, waves, tables, waves.shape, extra)
    tables = (*lane_fwd, *row_fwd, *last_rows, *lane_inv, *prop)
    cut = run_kernel(last_kernel, "slice_last", slabs[-1], waves, tables, (per_device, 2, quad_rows, crop), [])

    side = (place // 2) & 1
    pair = cut.reshape(per_device, 2, 2, quad_rows // 2, crop)
    kept = lax.dynamic_index_in_dim(pair, side, 2, False)
    other = flip(lax.dynamic_index_in_dim(pair, 1 - side, 2, False), 2, groups)
    both = jnp.stack([jnp.where(side == 0, kept, other), jnp.where(side == 0, other, kept)])
    side = place & 1
    pair = both.reshape(2, per_device, 2, 2, own_rows, crop)
    kept = lax.dynamic_index_in_dim(pair, side, 3, False)
    other = flip(lax.dynamic_index_in_dim(pair, 1 - side, 3, False), 1, groups)
    all_probes = jnp.stack([jnp.where(side == 0, kept, other), jnp.where(side == 0, other, kept)], axis=1)
    return jnp.transpose(all_probes.reshape(probes, 2, own_rows, crop), (2, 1, 0, 3))


def solution(mesh):
    placed = (P(("parts", "wide"), None, None), P("parts"), P(), P(), P("parts", None))
    return jax.shard_map(
        local,
        mesh=mesh,
        in_specs=placed,
        out_specs=P(("parts", "wide"), None, None, None),
        check_vma=False,
    )
```

```python
import functools
import math

import jax
import jax.numpy as jnp
import numpy as np
from jax import lax
from jax.experimental import pallas as pl
from jax.experimental.pallas import tpu as pltpu
from jax.sharding import PartitionSpec as P

FRESNEL = 4.7e-05
TWO_PI = 2.0 * math.pi
F32 = jnp.float32
BF16 = jnp.bfloat16
QUAD = 4
ROW_STEPS = 2


def flip(array, bit, groups):
    return lax.ppermute(array, "wide", [(i, i ^ bit) for i in range(groups)])


def half(array, which):
    rows = array.shape[0] // 2
    return lax.dynamic_slice_in_dim(array, which * rows, rows, 0)


def spread_slabs(own_slab, slice_owner, groups, device):
    count = slice_owner.shape[0]
    bits = [1 << b for b in range(groups.bit_length() - 1)]
    side = device & 1
    own = side
    kept = half(own_slab, side)
    received = flip(half(own_slab, 1 - side), 1, groups)
    zero = jnp.zeros_like(kept)
    parts = [
        jnp.where(slice_owner[s] == device, kept, jnp.where(slice_owner[s] == (device ^ 1), received, zero))
        for s in range(count)
    ]
    for bit in bits[1:-1]:
        side = (device // bit) & 1
        own = own * 2 + side
        parts = [half(part, side) + flip(half(part, 1 - side), bit, groups) for part in parts]
    parts = [part + flip(part, bits[-1], groups) for part in parts]
    for bit in reversed(bits[:-1]):
        parts = [jnp.concatenate([part, flip(part, bit, groups)], axis=0) for part in parts]
    return parts, own.astype(jnp.int32).reshape(1)


def class_frequencies(grid):
    top = grid // 3
    freq = np.zeros((4, grid // 4), np.int32)
    real = np.zeros((4, grid // 4), np.float32)
    longest = 0
    for c in range(4):
        members = [u for u in range(-top, top + 1) if u % 4 == c]
        freq[c, : len(members)] = members
        real[c, : len(members)] = 1.0
        longest = max(longest, len(members))
    return freq, real, -(-longest // 16) * 16


def cos_turns(turns, grid):
    turns = (turns + grid // 2) & (grid - 1)
    h = (turns - grid // 2).astype(F32) * (math.pi / grid)
    t = h * h
    p = -1.0 / math.factorial(11)
    for n in (9, 7, 5, 3, 1):
        p = p * t + (1.0 if n % 4 == 1 else -1.0) / math.factorial(n)
    s = h * p
    return 1.0 - 2.0 * (s * s)


def table_kernel(first_ref, cos_ref, sin_ref, rowf, lanef, lanew, lanep, wh, wl, vh, vl, pr, pi, dh, dl):
    q = cos_ref.shape[1]
    n = 4 * q
    kp = pr.shape[1]
    take = dh.shape[1] // 2
    for c in range(4):
        cos, sin = cos_ref[c], sin_ref[c]
        for a, b, part in ((0, 0, cos), (0, 1, -sin), (1, 0, sin), (1, 1, cos)):
            wh[c, a * q : (a + 1) * q, b * q : (b + 1) * q], wl[c, a * q : (a + 1) * q, b * q : (b + 1) * q] = split(part)
        cos, sin = cos.T, sin.T
        for a, b, part in ((0, 0, cos), (0, 1, sin), (1, 0, -sin), (1, 1, cos)):
            vh[c, a * q : (a + 1) * q, b * q : (b + 1) * q], vl[c, a * q : (a + 1) * q, b * q : (b + 1) * q] = split(part)
        for l in range(4):
            lanes = pl.ds(l * q, q)
            squared = rowf[c] + lanef[:, lanes]
            kept = 9.0 * squared <= float(n * n)
            re, im = cos_sin(jnp.where(kept, FRESNEL * squared, 0.0))
            pr[c, :, lanes] = jnp.where(kept, re * (1.0 / (n * n)), 0.0)
            pi[c, :, lanes] = jnp.where(kept, im * (-1.0 / (n * n)), 0.0)
        row = lax.broadcasted_iota(jnp.int32, (2 * take, 2 * q), 0)
        x = first_ref[0] + jnp.where(row < take, row, row - take)
        shift = lanep[...] - jnp.where(row < take, 0, n // 4)
        dh[c], dl[c] = split(cos_turns(x * lanew[c, 0] + shift, n) * lanew[c, 1].astype(F32))


def make_tables(grid, first_row, rows):
    freq, real, kp = class_frequencies(grid)
    q = grid // 4
    turns = np.mod(freq[:, None, :].astype(np.int64) * np.arange(q)[None, :, None], grid)
    angle = TWO_PI * turns / grid
    cos = (np.cos(angle) * real[:, None, :]).astype(np.float32)
    sin = (np.sin(angle) * real[:, None, :]).astype(np.float32)
    square = np.where(real > 0, freq.astype(np.float32) ** 2, float(grid * grid)).astype(np.float32)
    lane_pair = np.stack([np.tile(freq, (1, 2)), np.tile(real, (1, 2)).astype(np.int32)], axis=1)[:, :, None, :]
    lane_shift = np.repeat(np.array([0, grid // 4], np.int32), q)[None, :]
    inputs = (cos, sin, square[:, :kp, None], square.reshape(1, grid), lane_pair, lane_shift)
    inputs = [jnp.asarray(v) for v in inputs]
    full = jax.ShapeDtypeStruct((4, 2 * q, 2 * q), BF16)
    prop = jax.ShapeDtypeStruct((4, kp, grid), F32)
    last = jax.ShapeDtypeStruct((4, 2 * rows, 2 * q), BF16)
    vmem = pl.BlockSpec(memory_space=pltpu.VMEM)
    out = pl.pallas_call(
        table_kernel,
        name="tables",
        in_specs=[pl.BlockSpec(memory_space=pltpu.SMEM)] + [vmem] * len(inputs),
        out_specs=[vmem] * 8,
        out_shape=[full, full, full, full, prop, prop, last, last],
        compiler_params=pltpu.CompilerParams(vmem_limit_bytes=16 << 20),
    )(first_row.astype(jnp.int32).reshape(1), *inputs)
    return out[0:2], out[2:4], out[4:6], out[6:8]


def wave_kernel(row_freq, row_turn, row_weight, row_low, col_freq, col_turn, col_low, out_ref):
    n = out_ref.shape[2]
    k = row_freq.shape[1]

    def pick(value, low):
        high = value.astype(BF16).astype(F32)
        return jnp.where(low > 0, value - high, high).astype(BF16)

    x = lax.broadcasted_iota(jnp.int32, (n, k), 0)
    left = pick(cos_turns(x * row_freq[...] + row_turn[0], n) * row_weight[...], row_low[...])
    y = lax.broadcasted_iota(jnp.int32, (k, n), 1)
    for part in range(2):
        right = pick(cos_turns(y * col_freq[...] + col_turn[part], n), col_low[...])
        out_ref[0, part] = dot(left, right)


def probe_waves(grid, beam_index, aperture, position):
    beams = beam_index.shape[0]
    quarter = grid // 4
    zeros = np.zeros(beams, np.int32)
    k = 6 * beams
    row_freq = jnp.tile(beam_index[:, 0], 6).reshape(1, k)
    mixing = beam_index[:, 0][None, :] * position[:, 0][:, None] + beam_index[:, 1][None, :] * position[:, 1][:, None]
    row_turn = (np.tile(np.concatenate([zeros, zeros - quarter]), 3)[None, :] - jnp.tile(mixing, (1, 6)))[:, None, :]
    weight = jnp.tile(aperture.astype(F32) / math.sqrt(beams), 6).reshape(1, k)
    group = np.repeat(np.arange(3, dtype=np.int32), 2 * beams)
    col_freq = jnp.tile(beam_index[:, 1], 6).reshape(k, 1)
    col_turn = np.stack([np.tile(np.concatenate([zeros, zeros + quarter]), 3), np.tile(np.concatenate([zeros - quarter, zeros]), 3)])
    inputs = (row_freq, row_turn, weight, jnp.asarray((group == 1).astype(np.int32)[None, :]), col_freq, jnp.asarray(col_turn[:, :, None]), jnp.asarray((group == 2).astype(np.int32)[:, None]))
    shape = (position.shape[0], 2, grid, grid)
    specs = [whole(v) for v in inputs]
    specs[1] = one(row_turn.shape)
    return pl.pallas_call(
        wave_kernel,
        name="probe_waves",
        grid=(shape[0],),
        in_specs=specs,
        out_specs=one(shape),
        out_shape=jax.ShapeDtypeStruct(shape, F32),
        compiler_params=pltpu.CompilerParams(vmem_limit_bytes=16 << 20),
    )(*inputs)


def split(x):
    high = x.astype(BF16)
    return high, (x - high.astype(F32)).astype(BF16)


def dot(a, b):
    return jnp.dot(a, b, preferred_element_type=F32)


def dot3(ah, al, bh, bl):
    return dot(ah, bh) + dot(al, bh) + dot(ah, bl)


def butterfly(parts, sign):
    (r0, i0), (r1, i1), (r2, i2), (r3, i3) = parts
    sr, si, dr, di = r0 + r2, i0 + i2, r0 - r2, i0 - i2
    tr, ti, er, ei = r1 + r3, i1 + i3, r1 - r3, i1 - i3
    up = (dr - sign * ei, di + sign * er)
    down = (dr + sign * ei, di - sign * er)
    return [(sr + tr, si + ti), up, (sr - tr, si - ti), down]


def chebyshev(function, top, terms):
    fit = np.polynomial.chebyshev.Chebyshev.interpolate(function, terms - 1, domain=[0.0, top])
    return [float(v) for v in fit.convert(kind=np.polynomial.Polynomial).coef]


COS = chebyshev(lambda t: np.cos(np.sqrt(t)), 2.56, 5)
SIN = chebyshev(lambda t: np.sinc(np.sqrt(t) / np.pi), 2.56, 5)


def horner(coefficients, t):
    value = coefficients[-1]
    for coefficient in coefficients[-2::-1]:
        value = value * t + coefficient
    return value


def cos_sin(v):
    t = v * v
    return horner(COS, t), v * horner(SIN, t)


def transmit_tables(own_ref, slab_ref, tr_ref, ti_ref, blocks):
    n = slab_ref.shape[0]
    q = n // 4
    block_rows = n // blocks
    rows = min(32, block_rows)

    def body(b, carry):
        first = pl.multiple_of(b * rows, rows)
        place = ((first // block_rows) ^ own_ref[0]) * block_rows + first % block_rows
        place = pl.multiple_of(place, rows)
        for j in range(4):
            lanes = pl.ds(j * q, q)
            c, s = cos_sin(slab_ref[pl.ds(first, rows), lanes].astype(F32))
            tr_ref[pl.ds(place, rows), lanes] = c
            ti_ref[pl.ds(place, rows), lanes] = s
        return carry

    lax.fori_loop(0, n // rows, body, 0)


def forward(wave_ref, tr_ref, ti_ref, wh, wl, vh, vl, pr, pi, scratch, after):
    yh, yl, sr, si, zh, zl, uh, ul = scratch
    n = tr_ref.shape[0]
    q = n // 4
    kp = pr.shape[1]
    rows = 32

    def fold_lanes(first):
        at = pl.ds(first, rows)
        parts = []
        for j in range(4):
            lanes = pl.ds(j * q, q)
            wr, wi = wave_ref[0, 0, at, lanes], wave_ref[0, 1, at, lanes]
            cr, ci = tr_ref[at, lanes], ti_ref[at, lanes]
            parts.append((wr * cr - wi * ci, wr * ci + wi * cr))
        for c, (r, i) in enumerate(butterfly(parts, -1.0)):
            yh[c, at, :q], yl[c, at, :q] = split(r)
            yh[c, at, q:], yl[c, at, q:] = split(i)

    def fold_rows(l):
        lanes = pl.ds(l * q, q)
        for first in range(0, q, rows):
            parts = [(sr[pl.ds(j * q + first, rows), lanes], si[pl.ds(j * q + first, rows), lanes]) for j in range(4)]
            for c, (r, i) in enumerate(butterfly(parts, -1.0)):
                zh[c, pl.ds(first, rows), lanes], zl[c, pl.ds(first, rows), lanes] = split(r)
                zh[c, pl.ds(q + first, rows), lanes], zl[c, pl.ds(q + first, rows), lanes] = split(i)

    step = n // ROW_STEPS
    for b in range(ROW_STEPS):
        for first in range(b * step, (b + 1) * step, rows):
            fold_lanes(first)
        at = pl.ds(b * step, step)
        for c in range(4):
            out = dot3(yh[c, at], yl[c, at], wh[c], wl[c])
            sr[at, c * q : (c + 1) * q] = out[:, :q]
            si[at, c * q : (c + 1) * q] = out[:, q:]
            if b == ROW_STEPS - 1:
                fold_rows(c)
    for h in range(2):
        lanes = pl.ds(h * 2 * q, 2 * q)
        for c in range(4):
            zhc, zlc = zh[c, :, lanes], zl[c, :, lanes]
            r = dot3(vh[c, :kp], vl[c, :kp], zhc, zlc)
            i = dot3(vh[c, q : q + kp], vl[c, q : q + kp], zhc, zlc)
            re, im = pr[c, :, lanes], pi[c, :, lanes]
            uh[c, :kp, lanes], ul[c, :kp, lanes] = split(r * re - i * im)
            uh[c, q : q + kp, lanes], ul[c, q : q + kp, lanes] = split(r * im + i * re)
        after(h)


def first_kernel(blocks, own_ref, slab_ref, wave_ref, wh, wl, vh, vl, pr, pi, out_ref, tr, ti, yh, yl, sr, si, zh, zl, uh, ul, g, hr):
    n = slab_ref.shape[0]
    q = n // 4
    rows = 32

    @pl.when(pl.program_id(0) == 0)
    def _():
        transmit_tables(own_ref, slab_ref, tr, ti, blocks)
        uh[...] = jnp.zeros_like(uh)
        ul[...] = jnp.zeros_like(ul)

    def unfold_rows(l):
        lanes = pl.ds(l * q, q)
        for first in range(0, q, rows):
            parts = [(g[c, pl.ds(first, rows), lanes], g[c, pl.ds(q + first, rows), lanes]) for c in range(4)]
            for j, (r, i) in enumerate(butterfly(parts, 1.0)):
                at = pl.ds(j * q + first, rows)
                yh[l, at, :q], yl[l, at, :q] = split(r)
                yh[l, at, q:], yl[l, at, q:] = split(i)

    def after(h):
        lanes = pl.ds(h * 2 * q, 2 * q)
        for c in range(4):
            g[c, :, lanes] = dot3(wh[c], wl[c], uh[c, :, lanes], ul[c, :, lanes])
        for l in (2 * h, 2 * h + 1):
            unfold_rows(l)

    forward(wave_ref, tr, ti, wh, wl, vh, vl, pr, pi, (yh, yl, sr, si, zh, zl, uh, ul), after)
    step = n // ROW_STEPS
    for b in range(ROW_STEPS):
        at = pl.ds(b * step, step)
        for c in range(4):
            hr[c, at] = dot3(yh[c, at], yl[c, at], vh[c], vl[c])
        for first in range(b * step, (b + 1) * step, rows):
            at = pl.ds(first, rows)
            parts = [(hr[c, at, :q], hr[c, at, q:]) for c in range(4)]
            for j, (r, i) in enumerate(butterfly(parts, 1.0)):
                out_ref[0, 0, at, pl.ds(j * q, q)] = r
                out_ref[0, 1, at, pl.ds(j * q, q)] = i


def last_kernel(blocks, own_ref, slab_ref, wave_ref, wh, wl, vh, vl, pr, pi, dh, dl, out_ref, tr, ti, yh, yl, sr, si, zh, zl, uh, ul):
    n = slab_ref.shape[0]
    q = n // 4
    take = dh.shape[1] // 2

    @pl.when(pl.program_id(0) == 0)
    def _():
        transmit_tables(own_ref, slab_ref, tr, ti, blocks)
        uh[...] = jnp.zeros_like(uh)
        ul[...] = jnp.zeros_like(ul)

    half_out = []

    def after(h):
        lanes = pl.ds(h * 2 * q, 2 * q)
        out = dot3(dh[0], dl[0], uh[0, :, lanes], ul[0, :, lanes])
        for c in range(1, 4):
            out = out + dot3(dh[c], dl[c], uh[c, :, lanes], ul[c, :, lanes])
        half_out.append(out)

    forward(wave_ref, tr, ti, wh, wl, vh, vl, pr, pi, (yh, yl, sr, si, zh, zl, uh, ul), after)
    parts = []
    for c in range(4):
        lanes = slice(c % 2 * q, c % 2 * q + q)
        out = half_out[c // 2]
        high, low = split(jnp.concatenate([out[:take, lanes], out[take:, lanes]], axis=1))
        back = dot3(high, low, vh[c], vl[c])
        parts.append((back[:, :q], back[:, q:]))
    for j, (r, i) in enumerate(butterfly(parts, 1.0)[1:3]):
        out_ref[0, 0, :, j * q : (j + 1) * q] = r
        out_ref[0, 1, :, j * q : (j + 1) * q] = i


def whole(array):
    return pl.BlockSpec(array.shape, lambda p: (0,) * array.ndim, pipeline_mode=pl.Buffered(1))


def one(shape):
    return pl.BlockSpec((1,) + shape[1:], lambda p: (p,) + (0,) * (len(shape) - 1))


def forward_scratch(n):
    q = n // 4
    return [
        pltpu.VMEM((n, n), F32),
        pltpu.VMEM((n, n), F32),
        pltpu.VMEM((4, n, 2 * q), BF16),
        pltpu.VMEM((4, n, 2 * q), BF16),
        pltpu.VMEM((n, n), F32),
        pltpu.VMEM((n, n), F32),
        pltpu.VMEM((4, 2 * q, n), BF16),
        pltpu.VMEM((4, 2 * q, n), BF16),
        pltpu.VMEM((4, 2 * q, n), BF16),
        pltpu.VMEM((4, 2 * q, n), BF16),
    ]


def run_kernel(kernel, name, own, slab, waves, tables, out_shape, extra, blocks):
    n = slab.shape[0]
    return pl.pallas_call(
        functools.partial(kernel, blocks),
        name=name,
        grid=(waves.shape[0],),
        in_specs=[pl.BlockSpec(memory_space=pltpu.SMEM), whole(slab), one(waves.shape)] + [whole(t) for t in tables],
        out_specs=one(out_shape),
        out_shape=jax.ShapeDtypeStruct(out_shape, F32),
        scratch_shapes=forward_scratch(n) + extra,
        compiler_params=pltpu.CompilerParams(vmem_limit_bytes=40 << 20),
    )(own, slab, waves, *tables)


def local(potential_pool, slice_owner, beam_index, aperture, probe_position):
    grid = potential_pool.shape[-1]
    crop = grid // 2
    margin = grid // 4
    q = grid // 4
    groups = lax.axis_size("wide")
    device = lax.axis_index("wide")
    probes = probe_position.shape[0]
    per_device = probes // QUAD
    quad_rows = crop // (groups // QUAD)
    own_rows = crop // groups
    place = device % QUAD
    quad = device // QUAD

    slabs, own = spread_slabs(potential_pool[0], slice_owner, groups, device)
    blocks = groups // 2

    position = lax.dynamic_slice_in_dim(probe_position, place * per_device, per_device, 0)
    waves = probe_waves(grid, beam_index, aperture, position)
    forward_table, inverse_table, prop, last_rows = make_tables(grid, margin + quad * quad_rows, quad_rows)
    tables = (*forward_table, *inverse_table, *prop)

    for slab in slabs[:-1]:
        extra = [pltpu.VMEM((4, 2 * q, grid), F32), pltpu.VMEM((4, grid, 2 * q), F32)]
        waves = run_kernel(first_kernel, "slice_full", own, slab, waves, tables, waves.shape, extra, blocks)
    cut_shape = (per_device, 2, quad_rows, crop)
    cut = run_kernel(last_kernel, "slice_last", own, slabs[-1], waves, (*tables, *last_rows), cut_shape, [], blocks)

    side = (place // 2) & 1
    pair = cut.reshape(per_device, 2, 2, quad_rows // 2, crop)
    kept = lax.dynamic_index_in_dim(pair, side, 2, False)
    other = flip(lax.dynamic_index_in_dim(pair, 1 - side, 2, False), 2, groups)
    both = jnp.stack([jnp.where(side == 0, kept, other), jnp.where(side == 0, other, kept)])
    side = place & 1
    pair = both.reshape(2, per_device, 2, 2, own_rows, crop)
    kept = lax.dynamic_index_in_dim(pair, side, 3, False)
    other = flip(lax.dynamic_index_in_dim(pair, 1 - side, 3, False), 1, groups)
    all_probes = jnp.stack([jnp.where(side == 0, kept, other), jnp.where(side == 0, other, kept)], axis=1)
    return jnp.transpose(all_probes.reshape(probes, 2, own_rows, crop), (2, 1, 0, 3))


def solution(mesh):
    placed = (P(("parts", "wide"), None, None), P("parts"), P(), P(), P("parts", None))
    return jax.shard_map(
        local,
        mesh=mesh,
        in_specs=placed,
        out_specs=P(("parts", "wide"), None, None, None),
        check_vma=False,
    )
```

```python
import functools
import math

import jax
import jax.numpy as jnp
import numpy as np
from jax import lax
from jax.experimental import pallas as pl
from jax.experimental.pallas import tpu as pltpu
from jax.sharding import PartitionSpec as P


FRESNEL = 4.7e-05
F32 = jnp.float32
BF16 = jnp.bfloat16
QUAD = 4
ROW_STEPS = 2


def flip(array, bit, groups):
    return lax.ppermute(array, "wide", [(i, i ^ bit) for i in range(groups)])


def half(array, which):
    rows = array.shape[0] // 2
    return lax.dynamic_slice_in_dim(array, which * rows, rows, 0)


def spread_slabs(own_slab, slice_owner, groups, device):
    count = slice_owner.shape[0]
    bits = [1 << b for b in range(groups.bit_length() - 1)]
    side = device & 1
    own = side
    kept = half(own_slab, side)
    received = flip(half(own_slab, 1 - side), 1, groups)
    mine = (slice_owner == device)[:, None, None]
    theirs = (slice_owner == (device ^ 1))[:, None, None]
    picked = jnp.where(mine, kept, jnp.where(theirs, received, jnp.zeros_like(kept)))
    parts = [picked[s] for s in range(count)]
    for bit in bits[1:-1]:
        side = (device // bit) & 1
        own = own * 2 + side
        parts = [half(p, side) + flip(half(p, 1 - side), bit, groups) for p in parts]
    parts = [p + flip(p, bits[-1], groups) for p in parts]
    for bit in reversed(bits[2:-1]):
        parts = [jnp.concatenate([p, flip(p, bit, groups)], axis=0) for p in parts]
    pieces = []
    for part in parts:
        other = flip(part, 2, groups)
        pieces.append((part, other, flip(part, 1, groups), flip(other, 1, groups)))
    return pieces, own.astype(jnp.int32).reshape(1)


def class_frequencies(grid):
    top = grid // 3
    classes = [[u for u in range(-top, top + 1) if u % 4 == c] for c in range(4)]
    longest = max(len(c) for c in classes)
    return [(c[0], len(c)) for c in classes], -(-longest // 16) * 16


def cos_turns(turns, grid):
    turns = (turns + grid // 2) & (grid - 1)
    h = (turns - grid // 2).astype(F32) * (math.pi / grid)
    t = h * h
    p = -1.0 / math.factorial(11)
    for n in (9, 7, 5, 3, 1):
        p = p * t + (1.0 if n % 4 == 1 else -1.0) / math.factorial(n)
    s = h * p
    return 1.0 - 2.0 * (s * s)


def table_kernel(first_ref, wh, wl, vh, vl, pr, pi, dh, dl):
    q = wh.shape[1] // 2
    n = 4 * q
    kp = pr.shape[1]
    take = dh.shape[1] // 2
    classes, _ = class_frequencies(n)

    def iota(shape, axis):
        return lax.broadcasted_iota(jnp.int32, shape, axis)

    for c, (first, count) in enumerate(classes):
        lane = iota((q, q), 1)
        turn = iota((q, q), 0) * (first + 4 * lane)
        cos = jnp.where(lane < count, cos_turns(turn, n), 0.0)
        sin = jnp.where(lane < count, cos_turns(turn - n // 4, n), 0.0)
        for a, b, part in ((0, 0, cos), (0, 1, -sin), (1, 0, sin), (1, 1, cos)):
            wh[c, a * q : (a + 1) * q, b * q : (b + 1) * q], wl[c, a * q : (a + 1) * q, b * q : (b + 1) * q] = split(part)
        cos, sin = cos.T, sin.T
        for a, b, part in ((0, 0, cos), (0, 1, sin), (1, 0, -sin), (1, 1, cos)):
            vh[c, a * q : (a + 1) * q, b * q : (b + 1) * q], vl[c, a * q : (a + 1) * q, b * q : (b + 1) * q] = split(part)
        row, lane = iota((kp, q), 0), iota((kp, q), 1)
        for l, (first_l, count_l) in enumerate(classes):
            u, v = first + 4 * row, first_l + 4 * lane
            squared = u * u + v * v
            kept = (9 * squared <= n * n) & (row < count) & (lane < count_l)
            re, im = cos_sin(jnp.where(kept, FRESNEL * squared.astype(F32), 0.0))
            pr[c, :, l * q : (l + 1) * q] = jnp.where(kept, re * (1.0 / (n * n)), 0.0)
            pi[c, :, l * q : (l + 1) * q] = jnp.where(kept, im * (-1.0 / (n * n)), 0.0)
        lane = iota((take, q), 1)
        turn = (first_ref[0] + (iota((take, q), 0) ^ first_ref[1])) * (first + 4 * lane)
        cos = jnp.where(lane < count, cos_turns(turn, n), 0.0)
        sin = jnp.where(lane < count, cos_turns(turn - n // 4, n), 0.0)
        for a, b, part in ((0, 0, cos), (0, 1, -sin), (1, 0, sin), (1, 1, cos)):
            at = slice(a * take, (a + 1) * take)
            dh[c, at, b * q : (b + 1) * q], dl[c, at, b * q : (b + 1) * q] = split(part)


def make_tables(grid, first_row, order, rows):
    _, kp = class_frequencies(grid)
    q = grid // 4
    full = jax.ShapeDtypeStruct((4, 2 * q, 2 * q), BF16)
    prop = jax.ShapeDtypeStruct((4, kp, grid), F32)
    last = jax.ShapeDtypeStruct((4, 2 * rows, 2 * q), BF16)
    out = pl.pallas_call(
        table_kernel,
        name="tables",
        in_specs=[pl.BlockSpec(memory_space=pltpu.SMEM)],
        out_specs=[pl.BlockSpec(memory_space=pltpu.VMEM)] * 8,
        out_shape=[full, full, full, full, prop, prop, last, last],
        compiler_params=pltpu.CompilerParams(vmem_limit_bytes=12 << 20),
    )(jnp.stack([first_row, order]).astype(jnp.int32))
    return out[0:2], out[2:4], out[4:6], out[6:8]


def wave_kernel(place_ref, position_ref, beam_ref, left_ref, right_ref):
    probes, n, _ = left_ref.shape
    quarter = n // 4
    beams = beam_ref.shape[0]
    shift = beams.bit_length() - 1
    k = 6 * beams
    beam, position = beam_ref[...], position_ref[...]
    freq_x, freq_y, open_ = beam[:, 0:1], beam[:, 1:2], beam[:, 2:3]

    def part_group(index):
        return (index >> shift) & 1, index >> (shift + 1)

    lane = lax.broadcasted_iota(jnp.int32, (beams, k), 1)
    own = (lane & (beams - 1)) == lax.broadcasted_iota(jnp.int32, (beams, k), 0)

    def along_lanes(column):
        return jnp.sum(jnp.where(own, column.astype(F32), 0.0), axis=0, keepdims=True)

    def pick(value, low):
        high = value.astype(BF16).astype(F32)
        return jnp.where(low, value - high, high).astype(BF16)

    part, group = part_group(lax.broadcasted_iota(jnp.int32, (1, k), 1))
    row_freq = along_lanes(freq_x).astype(jnp.int32)
    weight = along_lanes(open_) * (1.0 / math.sqrt(beams))
    x = lax.broadcasted_iota(jnp.int32, (n, k), 0) * row_freq
    for p in range(probes):
        wanted = lax.broadcasted_iota(jnp.int32, position.shape, 0) == place_ref[0] * probes + p
        at = jnp.sum(jnp.where(wanted, position.astype(F32), 0.0), axis=0, keepdims=True).astype(jnp.int32)
        mixing = (freq_x * at[:, 0:1] + freq_y * at[:, 1:2]) & (n - 1)
        turn = -along_lanes(mixing).astype(jnp.int32) - quarter * part
        left_ref[p] = pick(cos_turns(x + turn, n) * weight, group == 1)
    part, group = part_group(lax.broadcasted_iota(jnp.int32, (k, n), 0))
    turn = lax.broadcasted_iota(jnp.int32, (k, n), 1) * jnp.concatenate([freq_y] * 6, axis=0)
    for c, extra in enumerate((quarter * part, quarter * part - quarter)):
        right_ref[c] = pick(cos_turns(turn + extra, n), group == 2)


def probe_waves(grid, beam_index, aperture, position, place):
    probes = position.shape[0] // QUAD
    k = 6 * beam_index.shape[0]
    beam = jnp.concatenate([beam_index, aperture[:, None]], axis=1)
    vmem = pl.BlockSpec(memory_space=pltpu.VMEM)
    return pl.pallas_call(
        wave_kernel,
        name="probe_waves",
        in_specs=[pl.BlockSpec(memory_space=pltpu.SMEM), vmem, vmem],
        out_specs=[vmem, vmem],
        out_shape=[jax.ShapeDtypeStruct((probes, grid, k), BF16), jax.ShapeDtypeStruct((2, k, grid), BF16)],
        compiler_params=pltpu.CompilerParams(vmem_limit_bytes=12 << 20),
    )(place.astype(jnp.int32).reshape(1), position, beam)


def split(x):
    high = x.astype(BF16)
    return high, (x - high.astype(F32)).astype(BF16)


def dot(a, b):
    return jnp.dot(a, b, preferred_element_type=F32)


def dot3(ah, al, bh, bl):
    return dot(ah, bh) + dot(al, bh) + dot(ah, bl)


def butterfly(parts, sign):
    (r0, i0), (r1, i1), (r2, i2), (r3, i3) = parts
    sr, si, dr, di = r0 + r2, i0 + i2, r0 - r2, i0 - i2
    tr, ti, er, ei = r1 + r3, i1 + i3, r1 - r3, i1 - i3
    up = (dr - sign * ei, di + sign * er)
    down = (dr + sign * ei, di - sign * er)
    return [(sr + tr, si + ti), up, (sr - tr, si - ti), down]


def chebyshev(function, top, terms):
    fit = np.polynomial.chebyshev.Chebyshev.interpolate(function, terms - 1, domain=[0.0, top])
    return [float(v) for v in fit.convert(kind=np.polynomial.Polynomial).coef]


COS = chebyshev(lambda t: np.cos(np.sqrt(t)), 2.56, 5)
SIN = chebyshev(lambda t: np.sinc(np.sqrt(t) / np.pi), 2.56, 5)


def horner(coefficients, t):
    value = coefficients[-1]
    for coefficient in coefficients[-2::-1]:
        value = value * t + coefficient
    return value


def cos_sin(v):
    t = v * v
    return horner(COS, t), v * horner(SIN, t)


def transmit_kernel(own_ref, *refs, blocks):
    pieces, (tr_ref, ti_ref) = refs[:-2], refs[-2:]
    block_rows = tr_ref.shape[0] // blocks
    each = blocks // len(pieces)
    for b in range(blocks):
        place = pl.multiple_of((own_ref[0] ^ b) * block_rows, block_rows)
        first = b % each * block_rows
        c, s = cos_sin(pieces[b // each][first : first + block_rows, :].astype(F32))
        tr_ref[pl.ds(place, block_rows), :] = c
        ti_ref[pl.ds(place, block_rows), :] = s


def transmit(own, pieces, blocks):
    vmem = pl.BlockSpec(memory_space=pltpu.VMEM)
    columns = pieces[0].shape[1]
    shape = jax.ShapeDtypeStruct((sum(piece.shape[0] for piece in pieces), columns), F32)
    return pl.pallas_call(
        functools.partial(transmit_kernel, blocks=blocks),
        name="transmit",
        in_specs=[pl.BlockSpec(memory_space=pltpu.SMEM)] + [vmem] * len(pieces),
        out_specs=[vmem, vmem],
        out_shape=[shape, shape],
        compiler_params=pltpu.CompilerParams(vmem_limit_bytes=8 << 20),
    )(own, *pieces)


def clear_padding(uh, ul, kp):
    q = uh.shape[1] // 2
    for spectrum in (uh, ul):
        for c in range(4):
            for first in (0, q):
                spectrum[c, first + kp : first + q] = jnp.zeros((q - kp, spectrum.shape[2]), BF16)


def forward(prepare, wave_ref, tr_ref, ti_ref, wh, wl, vh, vl, pr, pi, scratch, after):
    yh, yl, sr, si, zh, zl, uh, ul = scratch
    n = tr_ref.shape[0]
    q = n // 4
    kp = pr.shape[1]
    rows = 32

    def fold_lanes(first):
        at = pl.ds(first, rows)
        parts = []
        for j in range(4):
            lanes = pl.ds(j * q, q)
            wr, wi = wave_ref[0, at, lanes], wave_ref[1, at, lanes]
            cr, ci = tr_ref[at, lanes], ti_ref[at, lanes]
            parts.append((wr * cr - wi * ci, wr * ci + wi * cr))
        for c, (r, i) in enumerate(butterfly(parts, -1.0)):
            yh[c, at, :q], yl[c, at, :q] = split(r)
            yh[c, at, q:], yl[c, at, q:] = split(i)

    def fold_rows(l):
        lanes = pl.ds(l * q, q)
        for first in range(0, q, rows):
            parts = [(sr[pl.ds(j * q + first, rows), lanes], si[pl.ds(j * q + first, rows), lanes]) for j in range(4)]
            for c, (r, i) in enumerate(butterfly(parts, -1.0)):
                zh[c, pl.ds(first, rows), lanes], zl[c, pl.ds(first, rows), lanes] = split(r)
                zh[c, pl.ds(q + first, rows), lanes], zl[c, pl.ds(q + first, rows), lanes] = split(i)

    step = n // ROW_STEPS
    for b in range(ROW_STEPS):
        at = pl.ds(b * step, step)
        prepare(at)
        for first in range(b * step, (b + 1) * step, rows):
            fold_lanes(first)
        for c in range(4):
            out = dot3(yh[c, at], yl[c, at], wh[c], wl[c])
            sr[at, c * q : (c + 1) * q] = out[:, :q]
            si[at, c * q : (c + 1) * q] = out[:, q:]
            if b == ROW_STEPS - 1:
                fold_rows(c)
    for h in range(2):
        lanes = pl.ds(h * 2 * q, 2 * q)
        for c in range(4):
            zhc, zlc = zh[c, :, lanes], zl[c, :, lanes]
            r = dot3(vh[c, :kp], vl[c, :kp], zhc, zlc)
            i = dot3(vh[c, q : q + kp], vl[c, q : q + kp], zhc, zlc)
            re, im = pr[c, :, lanes], pi[c, :, lanes]
            uh[c, :kp, lanes], ul[c, :kp, lanes] = split(r * re - i * im)
            uh[c, q : q + kp, lanes], ul[c, q : q + kp, lanes] = split(r * im + i * re)
        after(h)


def first_kernel(probe, tr, ti, left_ref, right_ref, wh, wl, vh, vl, pr, pi, out_ref, wave_ref, *scratch):
    def prepare(at):
        for c in range(2):
            wave_ref[c, at] = dot(left_ref[probe, at], right_ref[c])

    slice_kernel(prepare, tr, ti, wave_ref, wh, wl, vh, vl, pr, pi, out_ref, *scratch)


def middle_kernel(tr, ti, wave_ref, wh, wl, vh, vl, pr, pi, out_ref, *scratch):
    slice_kernel(lambda at: None, tr, ti, wave_ref, wh, wl, vh, vl, pr, pi, out_ref, *scratch)


def slice_kernel(prepare, tr, ti, wave_ref, wh, wl, vh, vl, pr, pi, out_ref, yh, yl, sr, si, zh, zl, uh, ul, g, hr):
    n = tr.shape[0]
    q = n // 4
    rows = 32

    clear_padding(uh, ul, pr.shape[1])

    def unfold_rows(l):
        lanes = pl.ds(l * q, q)
        for first in range(0, q, rows):
            parts = [(g[c, pl.ds(first, rows), lanes], g[c, pl.ds(q + first, rows), lanes]) for c in range(4)]
            for j, (r, i) in enumerate(butterfly(parts, 1.0)):
                at = pl.ds(j * q + first, rows)
                yh[l, at, :q], yl[l, at, :q] = split(r)
                yh[l, at, q:], yl[l, at, q:] = split(i)

    def after(h):
        lanes = pl.ds(h * 2 * q, 2 * q)
        for c in range(4):
            g[c, :, lanes] = dot3(wh[c], wl[c], uh[c, :, lanes], ul[c, :, lanes])
        for l in (2 * h, 2 * h + 1):
            unfold_rows(l)

    forward(prepare, wave_ref, tr, ti, wh, wl, vh, vl, pr, pi, (yh, yl, sr, si, zh, zl, uh, ul), after)
    step = n // ROW_STEPS
    for b in range(ROW_STEPS):
        at = pl.ds(b * step, step)
        for c in range(4):
            hr[c, at] = dot3(yh[c, at], yl[c, at], vh[c], vl[c])
        for first in range(b * step, (b + 1) * step, rows):
            at = pl.ds(first, rows)
            parts = [(hr[c, at, :q], hr[c, at, q:]) for c in range(4)]
            for j, (r, i) in enumerate(butterfly(parts, 1.0)):
                out_ref[0, at, pl.ds(j * q, q)] = r
                out_ref[1, at, pl.ds(j * q, q)] = i


def last_kernel(tr, ti, wave_ref, wh, wl, vh, vl, pr, pi, dh, dl, keep_ref, away_ref, yh, yl, sr, si, zh, zl, uh, ul):
    n = tr.shape[0]
    q = n // 4
    take = dh.shape[1] // 2

    clear_padding(uh, ul, pr.shape[1])

    half_out = []

    def after(h):
        lanes = pl.ds(h * 2 * q, 2 * q)
        out = dot3(dh[0], dl[0], uh[0, :, lanes], ul[0, :, lanes])
        for c in range(1, 4):
            out = out + dot3(dh[c], dl[c], uh[c, :, lanes], ul[c, :, lanes])
        half_out.append(out)

    forward(lambda at: None, wave_ref, tr, ti, wh, wl, vh, vl, pr, pi, (yh, yl, sr, si, zh, zl, uh, ul), after)
    parts = []
    for c in range(4):
        lanes = slice(c % 2 * q, c % 2 * q + q)
        out = half_out[c // 2]
        high, low = split(jnp.concatenate([out[:take, lanes], out[take:, lanes]], axis=1))
        back = dot3(high, low, vh[c], vl[c])
        parts.append((back[:, :q], back[:, q:]))
    for j, (r, i) in enumerate(butterfly(parts, 1.0)[1:3]):
        for c, part in enumerate((r, i)):
            keep_ref[c, :, j * q : (j + 1) * q] = part[: take // 2]
            away_ref[c, :, j * q : (j + 1) * q] = part[take // 2 :]


def forward_scratch(n):
    q = n // 4
    return [
        pltpu.VMEM((4, n, 2 * q), BF16),
        pltpu.VMEM((4, n, 2 * q), BF16),
        pltpu.VMEM((n, n), F32),
        pltpu.VMEM((n, n), F32),
        pltpu.VMEM((4, 2 * q, n), BF16),
        pltpu.VMEM((4, 2 * q, n), BF16),
        pltpu.VMEM((4, 2 * q, n), BF16),
        pltpu.VMEM((4, 2 * q, n), BF16),
    ]


def run_kernel(kernel, inputs, out_shapes, first, extra):
    n = inputs[0].shape[-1]
    vmem = pl.BlockSpec(memory_space=pltpu.VMEM)
    return pl.pallas_call(
        kernel,
        in_specs=[vmem] * len(inputs),
        out_specs=[vmem] * len(out_shapes),
        out_shape=[jax.ShapeDtypeStruct(shape, F32) for shape in out_shapes],
        scratch_shapes=first + forward_scratch(n) + extra,
        compiler_params=pltpu.CompilerParams(vmem_limit_bytes=32 << 20),
    )(*inputs)


def local(potential_pool, slice_owner, beam_index, aperture, probe_position):
    grid = potential_pool.shape[-1]
    crop = grid // 2
    margin = grid // 4
    q = grid // 4
    groups = lax.axis_size("wide")
    device = lax.axis_index("wide")
    probes = probe_position.shape[0]
    per_device = probes // QUAD
    quad_rows = crop // (groups // QUAD)
    own_rows = crop // groups
    place = device % QUAD
    quad = device // QUAD

    slabs, own = spread_slabs(potential_pool[0], slice_owner, groups, device)
    blocks = groups // 2

    factors = probe_waves(grid, beam_index, aperture, probe_position, place)
    forward_table, inverse_table, prop, last_rows = make_tables(grid, margin + quad * quad_rows, place * own_rows, quad_rows)
    tables = (*forward_table, *inverse_table, *prop)
    extra = [pltpu.VMEM((4, 2 * q, grid), F32), pltpu.VMEM((4, grid, 2 * q), F32)]
    wave = [pltpu.VMEM((2, grid, grid), F32)]
    turned = transmit(own, slabs[0], blocks)
    waves = [
        run_kernel(functools.partial(first_kernel, p), (*turned, *factors, *tables), [(2, grid, grid)], wave, extra)[0]
        for p in range(per_device)
    ]
    for slab in slabs[1:-1]:
        turned = transmit(own, slab, blocks)
        waves = [run_kernel(middle_kernel, (*turned, w, *tables), [w.shape], [], extra)[0] for w in waves]
    turned = transmit(own, slabs[-1], blocks)

    kept, other = [], []
    for p in range(per_device):
        inputs = (*turned, waves[p], *tables, *last_rows)
        shape = (2, quad_rows // 2, crop)
        keep, away = run_kernel(last_kernel, inputs, [shape, shape], [], [])
        kept.append(keep)
        other.append(flip(away, 2, groups))
    pair = jnp.stack(kept + other)
    other = flip(pair[:, :, own_rows:], 1, groups)
    side_y, side_core = (place // 2) & 1, place & 1
    four = jnp.stack([pair[:, :, :own_rows], other]).reshape(2, 2, per_device, 2, own_rows, crop)
    four = jnp.where(side_core == 0, four, four[::-1])
    four = jnp.where(side_y == 0, four, four[:, ::-1])
    return jnp.transpose(four, (4, 3, 1, 0, 2, 5)).reshape(own_rows, 2, probes, crop)


def solution(mesh):
    placed = (P(("parts", "wide"), None, None), P("parts"), P(), P(), P("parts", None))

    return jax.shard_map(
        local,
        mesh=mesh,
        in_specs=placed,
        out_specs=P(("parts", "wide"), None, None, None),
        check_vma=False,
    )
```

```python
import functools
import math

import jax
import jax.numpy as jnp
import numpy as np
from jax import lax
from jax.experimental import pallas as pl
from jax.experimental.pallas import tpu as pltpu
from jax.sharding import PartitionSpec as P


FRESNEL = 4.7e-05
F32 = jnp.float32
BF16 = jnp.bfloat16
QUAD = 4
ROW_STEPS = 2


def flip(array, bit, groups):
    return lax.ppermute(array, "wide", [(i, i ^ bit) for i in range(groups)])


def half(array, which):
    rows = array.shape[0] // 2
    return lax.dynamic_slice_in_dim(array, which * rows, rows, 0)


def spread_slabs(own_slab, slice_owner, groups, device):
    count = slice_owner.shape[0]
    bits = [1 << b for b in range(groups.bit_length() - 1)]
    side = device & 1
    own = side
    kept = half(own_slab, side)
    received = flip(half(own_slab, 1 - side), 1, groups)
    mine = (slice_owner == device)[:, None, None]
    theirs = (slice_owner == (device ^ 1))[:, None, None]
    picked = jnp.where(mine, kept, jnp.where(theirs, received, jnp.zeros_like(kept)))
    parts = [picked[s] for s in range(count)]
    for bit in bits[1:-1]:
        side = (device // bit) & 1
        own = own * 2 + side
        parts = [half(p, side) + flip(half(p, 1 - side), bit, groups) for p in parts]
    parts = [p + flip(p, bits[-1], groups) for p in parts]
    for bit in reversed(bits[3:-1]):
        parts = [jnp.concatenate([p, flip(p, bit, groups)], axis=0) for p in parts]
    pieces = []
    for part in parts:
        grown = [part]
        for bit in reversed(bits[:3]):
            grown = grown + [flip(p, bit, groups) for p in grown]
        pieces.append(grown)
    return pieces, own.astype(jnp.int32).reshape(1)


def class_frequencies(grid):
    top = grid // 3
    classes = [[u for u in range(-top, top + 1) if u % 4 == c] for c in range(4)]
    longest = max(len(c) for c in classes)
    return [(c[0], len(c)) for c in classes], -(-longest // 16) * 16


def cos_turns(turns, grid):
    turns = (turns + grid // 2) & (grid - 1)
    h = (turns - grid // 2).astype(F32) * (math.pi / grid)
    t = h * h
    p = -1.0 / math.factorial(11)
    for n in (9, 7, 5, 3, 1):
        p = p * t + (1.0 if n % 4 == 1 else -1.0) / math.factorial(n)
    s = h * p
    return 1.0 - 2.0 * (s * s)


def table_kernel(wh, wl, vh, vl):
    q = wh.shape[1] // 2
    n = 4 * q
    classes, _ = class_frequencies(n)

    def iota(shape, axis):
        return lax.broadcasted_iota(jnp.int32, shape, axis)

    for c, (first, count) in enumerate(classes):
        lane = iota((q, q), 1)
        turn = iota((q, q), 0) * (first + 4 * lane)
        cos = jnp.where(lane < count, cos_turns(turn, n), 0.0)
        sin = jnp.where(lane < count, cos_turns(turn - n // 4, n), 0.0)
        for a, b, part in ((0, 0, cos), (0, 1, -sin), (1, 0, sin), (1, 1, cos)):
            wh[c, a * q : (a + 1) * q, b * q : (b + 1) * q], wl[c, a * q : (a + 1) * q, b * q : (b + 1) * q] = split(part)
        cos, sin = cos.T, sin.T
        for a, b, part in ((0, 0, cos), (0, 1, sin), (1, 0, -sin), (1, 1, cos)):
            vh[c, a * q : (a + 1) * q, b * q : (b + 1) * q], vl[c, a * q : (a + 1) * q, b * q : (b + 1) * q] = split(part)


def late_table_kernel(first_ref, pr, pi, dh, dl):
    q = dh.shape[2] // 2
    n = 4 * q
    kp = pr.shape[1]
    take = dh.shape[1] // 2
    classes, _ = class_frequencies(n)

    def iota(shape, axis):
        return lax.broadcasted_iota(jnp.int32, shape, axis)

    for c, (first, count) in enumerate(classes):
        row, lane = iota((kp, q), 0), iota((kp, q), 1)
        for l, (first_l, count_l) in enumerate(classes):
            u, v = first + 4 * row, first_l + 4 * lane
            squared = u * u + v * v
            kept = (9 * squared <= n * n) & (row < count) & (lane < count_l)
            re, im = cos_sin(jnp.where(kept, FRESNEL * squared.astype(F32), 0.0))
            pr[c, :, l * q : (l + 1) * q] = jnp.where(kept, re * (1.0 / (n * n)), 0.0)
            pi[c, :, l * q : (l + 1) * q] = jnp.where(kept, im * (-1.0 / (n * n)), 0.0)
        lane = iota((take, q), 1)
        turn = (first_ref[0] + (iota((take, q), 0) ^ first_ref[1])) * (first + 4 * lane)
        cos = jnp.where(lane < count, cos_turns(turn, n), 0.0)
        sin = jnp.where(lane < count, cos_turns(turn - n // 4, n), 0.0)
        for a, b, part in ((0, 0, cos), (0, 1, -sin), (1, 0, sin), (1, 1, cos)):
            at = slice(a * take, (a + 1) * take)
            dh[c, at, b * q : (b + 1) * q], dl[c, at, b * q : (b + 1) * q] = split(part)


def make_tables(grid, first_row, order, rows):
    _, kp = class_frequencies(grid)
    q = grid // 4
    full = jax.ShapeDtypeStruct((4, 2 * q, 2 * q), BF16)
    prop = jax.ShapeDtypeStruct((4, kp, grid), F32)
    last = jax.ShapeDtypeStruct((4, 2 * rows, 2 * q), BF16)
    vmem = pl.BlockSpec(memory_space=pltpu.VMEM)
    params = pltpu.CompilerParams(vmem_limit_bytes=12 << 20)
    out = pl.pallas_call(
        table_kernel,
        name="tables",
        out_specs=[vmem] * 4,
        out_shape=[full] * 4,
        compiler_params=params,
    )()
    late = pl.pallas_call(
        late_table_kernel,
        name="late_tables",
        in_specs=[pl.BlockSpec(memory_space=pltpu.SMEM)],
        out_specs=[vmem] * 4,
        out_shape=[prop, prop, last, last],
        compiler_params=params,
    )(jnp.stack([first_row, order]).astype(jnp.int32))
    return out[0:2], out[2:4], late[0:2], late[2:4]


def wave_kernel(place_ref, position_ref, beam_ref, left_ref, right_ref):
    probes, n, _ = left_ref.shape
    quarter = n // 4
    beams = beam_ref.shape[0]
    shift = beams.bit_length() - 1
    k = 6 * beams
    beam, position = beam_ref[...], position_ref[...]
    freq_x, freq_y, open_ = beam[:, 0:1], beam[:, 1:2], beam[:, 2:3]

    def part_group(index):
        return (index >> shift) & 1, index >> (shift + 1)

    lane = lax.broadcasted_iota(jnp.int32, (beams, k), 1)
    own = (lane & (beams - 1)) == lax.broadcasted_iota(jnp.int32, (beams, k), 0)

    def along_lanes(column):
        return jnp.sum(jnp.where(own, column.astype(F32), 0.0), axis=0, keepdims=True)

    def pick(value, low):
        high = value.astype(BF16).astype(F32)
        return jnp.where(low, value - high, high).astype(BF16)

    part, group = part_group(lax.broadcasted_iota(jnp.int32, (1, k), 1))
    row_freq = along_lanes(freq_x).astype(jnp.int32)
    weight = along_lanes(open_) * (1.0 / math.sqrt(beams))
    x = lax.broadcasted_iota(jnp.int32, (n, k), 0) * row_freq
    for p in range(probes):
        wanted = lax.broadcasted_iota(jnp.int32, position.shape, 0) == place_ref[0] * probes + p
        at = jnp.sum(jnp.where(wanted, position.astype(F32), 0.0), axis=0, keepdims=True).astype(jnp.int32)
        mixing = (freq_x * at[:, 0:1] + freq_y * at[:, 1:2]) & (n - 1)
        turn = -along_lanes(mixing).astype(jnp.int32) - quarter * part
        left_ref[p] = pick(cos_turns(x + turn, n) * weight, group == 1)
    part, group = part_group(lax.broadcasted_iota(jnp.int32, (k, n), 0))
    turn = lax.broadcasted_iota(jnp.int32, (k, n), 1) * jnp.concatenate([freq_y] * 6, axis=0)
    for c, extra in enumerate((quarter * part, quarter * part - quarter)):
        right_ref[c] = pick(cos_turns(turn + extra, n), group == 2)


def probe_waves(grid, beam_index, aperture, position, place):
    probes = position.shape[0] // QUAD
    k = 6 * beam_index.shape[0]
    beam = jnp.concatenate([beam_index, aperture[:, None]], axis=1)
    vmem = pl.BlockSpec(memory_space=pltpu.VMEM)
    return pl.pallas_call(
        wave_kernel,
        name="probe_waves",
        in_specs=[pl.BlockSpec(memory_space=pltpu.SMEM), vmem, vmem],
        out_specs=[vmem, vmem],
        out_shape=[jax.ShapeDtypeStruct((probes, grid, k), BF16), jax.ShapeDtypeStruct((2, k, grid), BF16)],
        compiler_params=pltpu.CompilerParams(vmem_limit_bytes=12 << 20),
    )(place.astype(jnp.int32).reshape(1), position, beam)


def split(x):
    high = x.astype(BF16)
    return high, (x - high.astype(F32)).astype(BF16)


def dot(a, b):
    return jnp.dot(a, b, preferred_element_type=F32)


def dot3(ah, al, bh, bl):
    return dot(ah, bh) + dot(al, bh) + dot(ah, bl)


def butterfly(parts, sign):
    (r0, i0), (r1, i1), (r2, i2), (r3, i3) = parts
    sr, si, dr, di = r0 + r2, i0 + i2, r0 - r2, i0 - i2
    tr, ti, er, ei = r1 + r3, i1 + i3, r1 - r3, i1 - i3
    up = (dr - sign * ei, di + sign * er)
    down = (dr + sign * ei, di - sign * er)
    return [(sr + tr, si + ti), up, (sr - tr, si - ti), down]


def chebyshev(function, top, terms):
    fit = np.polynomial.chebyshev.Chebyshev.interpolate(function, terms - 1, domain=[0.0, top])
    return [float(v) for v in fit.convert(kind=np.polynomial.Polynomial).coef]


COS = chebyshev(lambda t: np.cos(np.sqrt(t)), 2.56, 5)
SIN = chebyshev(lambda t: np.sinc(np.sqrt(t) / np.pi), 2.56, 5)


def horner(coefficients, t):
    value = coefficients[-1]
    for coefficient in coefficients[-2::-1]:
        value = value * t + coefficient
    return value


def cos_sin(v):
    t = v * v
    return horner(COS, t), v * horner(SIN, t)


def transmit_kernel(own_ref, *refs, blocks):
    pieces, (tr_ref, ti_ref) = refs[:-2], refs[-2:]
    block_rows = tr_ref.shape[0] // blocks
    each = blocks // len(pieces)
    for b in range(blocks):
        place = pl.multiple_of((own_ref[0] ^ b) * block_rows, block_rows)
        first = b % each * block_rows
        c, s = cos_sin(pieces[b // each][first : first + block_rows, :].astype(F32))
        tr_ref[pl.ds(place, block_rows), :] = c
        ti_ref[pl.ds(place, block_rows), :] = s


def transmit(own, pieces, blocks):
    vmem = pl.BlockSpec(memory_space=pltpu.VMEM)
    columns = pieces[0].shape[1]
    shape = jax.ShapeDtypeStruct((sum(piece.shape[0] for piece in pieces), columns), F32)
    return pl.pallas_call(
        functools.partial(transmit_kernel, blocks=blocks),
        name="transmit",
        in_specs=[pl.BlockSpec(memory_space=pltpu.SMEM)] + [vmem] * len(pieces),
        out_specs=[vmem, vmem],
        out_shape=[shape, shape],
        compiler_params=pltpu.CompilerParams(vmem_limit_bytes=8 << 20),
    )(own, *pieces)


def clear_padding(uh, ul, kp):
    q = uh.shape[1] // 2
    for spectrum in (uh, ul):
        for c in range(4):
            for first in (0, q):
                spectrum[c, first + kp : first + q] = jnp.zeros((q - kp, spectrum.shape[2]), BF16)


def forward(prepare, wave_ref, tr_ref, ti_ref, wh, wl, vh, vl, pr, pi, scratch, after):
    yh, yl, sr, si, zh, zl, uh, ul = scratch
    n = tr_ref.shape[0]
    q = n // 4
    kp = pr.shape[1]
    rows = 32

    def fold_lanes(first):
        at = pl.ds(first, rows)
        parts = []
        for j in range(4):
            lanes = pl.ds(j * q, q)
            wr, wi = wave_ref[0, at, lanes], wave_ref[1, at, lanes]
            cr, ci = tr_ref[at, lanes], ti_ref[at, lanes]
            parts.append((wr * cr - wi * ci, wr * ci + wi * cr))
        for c, (r, i) in enumerate(butterfly(parts, -1.0)):
            yh[c, at, :q], yl[c, at, :q] = split(r)
            yh[c, at, q:], yl[c, at, q:] = split(i)

    def fold_rows(l):
        lanes = pl.ds(l * q, q)
        for first in range(0, q, rows):
            parts = [(sr[pl.ds(j * q + first, rows), lanes], si[pl.ds(j * q + first, rows), lanes]) for j in range(4)]
            for c, (r, i) in enumerate(butterfly(parts, -1.0)):
                zh[c, pl.ds(first, rows), lanes], zl[c, pl.ds(first, rows), lanes] = split(r)
                zh[c, pl.ds(q + first, rows), lanes], zl[c, pl.ds(q + first, rows), lanes] = split(i)

    step = n // ROW_STEPS
    for b in range(ROW_STEPS):
        at = pl.ds(b * step, step)
        prepare(at)
        for first in range(b * step, (b + 1) * step, rows):
            fold_lanes(first)
        for c in range(4):
            out = dot3(yh[c, at], yl[c, at], wh[c], wl[c])
            sr[at, c * q : (c + 1) * q] = out[:, :q]
            si[at, c * q : (c + 1) * q] = out[:, q:]
            if b == ROW_STEPS - 1:
                fold_rows(c)
    for h in range(2):
        lanes = pl.ds(h * 2 * q, 2 * q)
        for c in range(4):
            zhc, zlc = zh[c, :, lanes], zl[c, :, lanes]
            r = dot3(vh[c, :kp], vl[c, :kp], zhc, zlc)
            i = dot3(vh[c, q : q + kp], vl[c, q : q + kp], zhc, zlc)
            re, im = pr[c, :, lanes], pi[c, :, lanes]
            uh[c, :kp, lanes], ul[c, :kp, lanes] = split(r * re - i * im)
            uh[c, q : q + kp, lanes], ul[c, q : q + kp, lanes] = split(r * im + i * re)
        after(h)


def first_kernel(probe, tr, ti, left_ref, right_ref, wh, wl, vh, vl, pr, pi, out_ref, wave_ref, *scratch):
    def prepare(at):
        for c in range(2):
            wave_ref[c, at] = dot(left_ref[probe, at], right_ref[c])

    slice_kernel(prepare, tr, ti, wave_ref, wh, wl, vh, vl, pr, pi, out_ref, *scratch)


def middle_kernel(tr, ti, wave_ref, wh, wl, vh, vl, pr, pi, out_ref, *scratch):
    slice_kernel(lambda at: None, tr, ti, wave_ref, wh, wl, vh, vl, pr, pi, out_ref, *scratch)


def slice_kernel(prepare, tr, ti, wave_ref, wh, wl, vh, vl, pr, pi, out_ref, yh, yl, sr, si, zh, zl, uh, ul, g, hr):
    n = tr.shape[0]
    q = n // 4
    rows = 32

    clear_padding(uh, ul, pr.shape[1])

    def unfold_rows(l):
        lanes = pl.ds(l * q, q)
        for first in range(0, q, rows):
            parts = [(g[c, pl.ds(first, rows), lanes], g[c, pl.ds(q + first, rows), lanes]) for c in range(4)]
            for j, (r, i) in enumerate(butterfly(parts, 1.0)):
                at = pl.ds(j * q + first, rows)
                yh[l, at, :q], yl[l, at, :q] = split(r)
                yh[l, at, q:], yl[l, at, q:] = split(i)

    def after(h):
        lanes = pl.ds(h * 2 * q, 2 * q)
        for c in range(4):
            g[c, :, lanes] = dot3(wh[c], wl[c], uh[c, :, lanes], ul[c, :, lanes])
        for l in (2 * h, 2 * h + 1):
            unfold_rows(l)

    forward(prepare, wave_ref, tr, ti, wh, wl, vh, vl, pr, pi, (yh, yl, sr, si, zh, zl, uh, ul), after)
    step = n // ROW_STEPS
    for b in range(ROW_STEPS):
        at = pl.ds(b * step, step)
        for c in range(4):
            hr[c, at] = dot3(yh[c, at], yl[c, at], vh[c], vl[c])
        for first in range(b * step, (b + 1) * step, rows):
            at = pl.ds(first, rows)
            parts = [(hr[c, at, :q], hr[c, at, q:]) for c in range(4)]
            for j, (r, i) in enumerate(butterfly(parts, 1.0)):
                out_ref[0, at, pl.ds(j * q, q)] = r
                out_ref[1, at, pl.ds(j * q, q)] = i


def last_kernel(probes, tr, ti, *refs):
    waves, (wh, wl, vh, vl, pr, pi, dh, dl, keep_ref, away_ref) = refs[:probes], refs[probes : probes + 10]
    scratch = refs[probes + 10 :]
    each = len(scratch) // probes
    for p in range(probes):
        own = scratch[p * each : (p + 1) * each]
        last_one(tr, ti, waves[p], wh, wl, vh, vl, pr, pi, dh, dl, keep_ref.at[p], away_ref.at[p], *own)


def last_one(tr, ti, wave_ref, wh, wl, vh, vl, pr, pi, dh, dl, keep_ref, away_ref, yh, yl, sr, si, zh, zl, uh, ul):
    n = tr.shape[0]
    q = n // 4
    take = dh.shape[1] // 2

    clear_padding(uh, ul, pr.shape[1])

    half_out = []

    def after(h):
        lanes = pl.ds(h * 2 * q, 2 * q)
        out = dot3(dh[0], dl[0], uh[0, :, lanes], ul[0, :, lanes])
        for c in range(1, 4):
            out = out + dot3(dh[c], dl[c], uh[c, :, lanes], ul[c, :, lanes])
        half_out.append(out)

    forward(lambda at: None, wave_ref, tr, ti, wh, wl, vh, vl, pr, pi, (yh, yl, sr, si, zh, zl, uh, ul), after)
    parts = []
    for c in range(4):
        lanes = slice(c % 2 * q, c % 2 * q + q)
        out = half_out[c // 2]
        high, low = split(jnp.concatenate([out[:take, lanes], out[take:, lanes]], axis=1))
        back = dot3(high, low, vh[c], vl[c])
        parts.append((back[:, :q], back[:, q:]))
    for j, (r, i) in enumerate(butterfly(parts, 1.0)[1:3]):
        for c, part in enumerate((r, i)):
            keep_ref[c, :, j * q : (j + 1) * q] = part[: take // 2]
            away_ref[c, :, j * q : (j + 1) * q] = part[take // 2 :]


def gather_kernel(place_ref, pair_ref, other_ref, out_ref, buffer):
    rows, _, probes, _ = out_ref.shape
    per_device = probes // QUAD
    for y in range(2):
        for core in range(2):
            slot = (place_ref[0] ^ (2 * y + core)) * per_device
            for p in range(per_device):
                source = other_ref[y * per_device + p] if core else pair_ref[y * per_device + p, :, :rows]
                buffer[slot + p] = source
    for r in range(rows):
        for c in range(2):
            out_ref[r, c] = buffer[:, c, r, :]


def forward_scratch(n):
    q = n // 4
    return [
        pltpu.VMEM((4, n, 2 * q), BF16),
        pltpu.VMEM((4, n, 2 * q), BF16),
        pltpu.VMEM((n, n), F32),
        pltpu.VMEM((n, n), F32),
        pltpu.VMEM((4, 2 * q, n), BF16),
        pltpu.VMEM((4, 2 * q, n), BF16),
        pltpu.VMEM((4, 2 * q, n), BF16),
        pltpu.VMEM((4, 2 * q, n), BF16),
    ]


def run_kernel(kernel, inputs, out_shapes, first, extra):
    n = inputs[0].shape[-1]
    vmem = pl.BlockSpec(memory_space=pltpu.VMEM)
    return pl.pallas_call(
        kernel,
        in_specs=[vmem] * len(inputs),
        out_specs=[vmem] * len(out_shapes),
        out_shape=[jax.ShapeDtypeStruct(shape, F32) for shape in out_shapes],
        scratch_shapes=first + forward_scratch(n) + extra,
        compiler_params=pltpu.CompilerParams(vmem_limit_bytes=36 << 20),
    )(*inputs)


def local(potential_pool, slice_owner, beam_index, aperture, probe_position):
    grid = potential_pool.shape[-1]
    crop = grid // 2
    margin = grid // 4
    q = grid // 4
    groups = lax.axis_size("wide")
    device = lax.axis_index("wide")
    probes = probe_position.shape[0]
    per_device = probes // QUAD
    quad_rows = crop // (groups // QUAD)
    own_rows = crop // groups
    place = device % QUAD
    quad = device // QUAD

    slabs, own = spread_slabs(potential_pool[0], slice_owner, groups, device)
    blocks = groups // 2

    factors = probe_waves(grid, beam_index, aperture, probe_position, place)
    forward_table, inverse_table, prop, last_rows = make_tables(grid, margin + quad * quad_rows, place * own_rows, quad_rows)
    tables = (*forward_table, *inverse_table, *prop)
    extra = [pltpu.VMEM((4, 2 * q, grid), F32), pltpu.VMEM((4, grid, 2 * q), F32)]
    wave = [pltpu.VMEM((2, grid, grid), F32)]
    turned = transmit(own, slabs[0], blocks)
    waves = [
        run_kernel(functools.partial(first_kernel, p), (*turned, *factors, *tables), [(2, grid, grid)], wave, extra)[0]
        for p in range(per_device)
    ]
    for slab in slabs[1:-1]:
        turned = transmit(own, slab, blocks)
        waves = [run_kernel(middle_kernel, (*turned, w, *tables), [w.shape], [], extra)[0] for w in waves]
    turned = transmit(own, slabs[-1], blocks)

    inputs = (*turned, *waves, *tables, *last_rows)
    shape = (per_device, 2, quad_rows // 2, crop)
    more = forward_scratch(grid) * (per_device - 1)
    keep, away = run_kernel(functools.partial(last_kernel, per_device), inputs, [shape, shape], [], more)
    pair = jnp.concatenate([keep, flip(away, 2, groups)], axis=0)
    other = flip(pair[:, :, own_rows:], 1, groups)
    vmem = pl.BlockSpec(memory_space=pltpu.VMEM)
    return pl.pallas_call(
        gather_kernel,
        name="gather_probes",
        in_specs=[pl.BlockSpec(memory_space=pltpu.SMEM), vmem, vmem],
        out_specs=vmem,
        out_shape=jax.ShapeDtypeStruct((own_rows, 2, probes, crop), F32),
        scratch_shapes=[pltpu.VMEM((probes, 2, own_rows, crop), F32)],
        compiler_params=pltpu.CompilerParams(vmem_limit_bytes=8 << 20),
    )(place.astype(jnp.int32).reshape(1), pair, other)


def solution(mesh):
    placed = (P(("parts", "wide"), None, None), P("parts"), P(), P(), P("parts", None))

    return jax.shard_map(
        local,
        mesh=mesh,
        in_specs=placed,
        out_specs=P(("parts", "wide"), None, None, None),
        check_vma=False,
    )
```

```python
import functools
import math

import jax
import jax.numpy as jnp
import numpy as np
from jax import lax
from jax.experimental import pallas as pl
from jax.experimental.pallas import tpu as pltpu
from jax.sharding import PartitionSpec as P


FRESNEL = 4.7e-05
F32 = jnp.float32
BF16 = jnp.bfloat16
QUAD = 4
ROW_STEPS = 2


def flip(array, bit, groups):
    return lax.ppermute(array, "wide", [(i, i ^ bit) for i in range(groups)])


def half(array, which):
    rows = array.shape[0] // 2
    return lax.dynamic_slice_in_dim(array, which * rows, rows, 0)


def spread_slabs(own_slab, slice_owner, groups, device):
    count = slice_owner.shape[0]
    bits = [1 << b for b in range(groups.bit_length() - 1)]
    side = device & 1
    own = side
    kept = half(own_slab, side)
    received = half(flip(own_slab, 1, groups), side)
    mine = (slice_owner == device)[:, None, None]
    theirs = (slice_owner == (device ^ 1))[:, None, None]
    picked = jnp.where(mine, kept, jnp.where(theirs, received, jnp.zeros_like(kept)))
    parts = [picked[s] for s in range(count)]
    for bit in bits[1:-1]:
        side = (device // bit) & 1
        own = own * 2 + side
        parts = [half(p, side) + flip(half(p, 1 - side), bit, groups) for p in parts]
    parts = [p + flip(p, bits[-1], groups) for p in parts]
    for bit in reversed(bits[3:-1]):
        parts = [jnp.concatenate([p, flip(p, bit, groups)], axis=0) for p in parts]
    pieces = []
    for part in parts:
        grown = [part]
        for bit in reversed(bits[:3]):
            grown = grown + [flip(p, bit, groups) for p in grown]
        pieces.append(grown)
    return pieces, own.astype(jnp.int32).reshape(1)


def class_frequencies(grid):
    top = grid // 3
    classes = [[u for u in range(-top, top + 1) if u % 4 == c] for c in range(4)]
    longest = max(len(c) for c in classes)
    return [(c[0], len(c)) for c in classes[:3]], -(-longest // 16) * 16


def signed(c, sin):
    return ((1, sin), (3, -sin)) if c == 1 else ((c, sin),)


def cos_turns(turns, grid):
    turns = (turns + grid // 2) & (grid - 1)
    h = (turns - grid // 2).astype(F32) * (math.pi / grid)
    t = h * h
    p = -1.0 / math.factorial(11)
    for n in (9, 7, 5, 3, 1):
        p = p * t + (1.0 if n % 4 == 1 else -1.0) / math.factorial(n)
    s = h * p
    return 1.0 - 2.0 * (s * s)


def table_kernel(wh, wl, vh, vl):
    q = wh.shape[1] // 2
    n = 4 * q
    classes, _ = class_frequencies(n)

    def iota(shape, axis):
        return lax.broadcasted_iota(jnp.int32, shape, axis)

    for c, (first, count) in enumerate(classes):
        lane = iota((q, q), 1)
        turn = iota((q, q), 0) * (first + 4 * lane)
        cos = jnp.where(lane < count, cos_turns(turn, n), 0.0)
        sin = jnp.where(lane < count, cos_turns(turn - n // 4, n), 0.0)
        for k, sine in signed(c, sin):
            for a, b, part in ((0, 0, cos), (0, 1, -sine), (1, 0, sine), (1, 1, cos)):
                at = (k, slice(a * q, (a + 1) * q), slice(b * q, (b + 1) * q))
                wh[at], wl[at] = split(part)
        cos, sin = cos.T, sin.T
        for k, sine in signed(c, sin):
            for a, b, part in ((0, 0, cos), (0, 1, sine), (1, 0, -sine), (1, 1, cos)):
                at = (k, slice(a * q, (a + 1) * q), slice(b * q, (b + 1) * q))
                vh[at], vl[at] = split(part)


def late_table_kernel(first_ref, pr, pi, dh, dl):
    q = dh.shape[2] // 2
    n = 4 * q
    kp = pr.shape[1]
    take = dh.shape[1] // 2
    classes, _ = class_frequencies(n)

    def iota(shape, axis):
        return lax.broadcasted_iota(jnp.int32, shape, axis)

    for c, (first, count) in enumerate(classes):
        row, lane = iota((kp, q), 0), iota((kp, q), 1)
        for l, (first_l, count_l) in enumerate(classes):
            u, v = first + 4 * row, first_l + 4 * lane
            squared = u * u + v * v
            kept = (9 * squared <= n * n) & (row < count) & (lane < count_l)
            re, im = cos_sin(jnp.where(kept, FRESNEL * squared.astype(F32), 0.0))
            re, im = jnp.where(kept, re * (1.0 / (n * n)), 0.0), jnp.where(kept, im * (-1.0 / (n * n)), 0.0)
            for k in (1, 3) if l == 1 else (l,):
                pr[c, :, k * q : (k + 1) * q] = re
                pi[c, :, k * q : (k + 1) * q] = im
        lane = iota((take, q), 1)
        turn = (first_ref[0] + (iota((take, q), 0) ^ first_ref[1])) * (first + 4 * lane)
        cos = jnp.where(lane < count, cos_turns(turn, n), 0.0)
        sin = jnp.where(lane < count, cos_turns(turn - n // 4, n), 0.0)
        for k, sine in signed(c, sin):
            for a, b, part in ((0, 0, cos), (0, 1, -sine), (1, 0, sine), (1, 1, cos)):
                at = (k, slice(a * take, (a + 1) * take), slice(b * q, (b + 1) * q))
                dh[at], dl[at] = split(part)


def make_tables(grid, first_row, order, rows):
    _, kp = class_frequencies(grid)
    q = grid // 4
    full = jax.ShapeDtypeStruct((4, 2 * q, 2 * q), BF16)
    prop = jax.ShapeDtypeStruct((3, kp, grid), F32)
    last = jax.ShapeDtypeStruct((4, 2 * rows, 2 * q), BF16)
    vmem = pl.BlockSpec(memory_space=pltpu.VMEM)
    params = pltpu.CompilerParams(vmem_limit_bytes=12 << 20)
    out = pl.pallas_call(
        table_kernel,
        name="tables",
        out_specs=[vmem] * 4,
        out_shape=[full] * 4,
        compiler_params=params,
    )()
    late = pl.pallas_call(
        late_table_kernel,
        name="late_tables",
        in_specs=[pl.BlockSpec(memory_space=pltpu.SMEM)],
        out_specs=[vmem] * 4,
        out_shape=[prop, prop, last, last],
        compiler_params=params,
    )(jnp.stack([first_row, order]).astype(jnp.int32))
    return out[0:2], out[2:4], late[0:2], late[2:4]


def wave_kernel(place_ref, position_ref, beam_ref, left_ref, right_ref):
    probes, n, _ = left_ref.shape
    quarter = n // 4
    beams = beam_ref.shape[0]
    shift = beams.bit_length() - 1
    k = 6 * beams
    beam, position = beam_ref[...], position_ref[...]
    freq_x, freq_y, open_ = beam[:, 0:1], beam[:, 1:2], beam[:, 2:3]

    def part_group(index):
        return (index >> shift) & 1, index >> (shift + 1)

    lane = lax.broadcasted_iota(jnp.int32, (beams, k), 1)
    own = (lane & (beams - 1)) == lax.broadcasted_iota(jnp.int32, (beams, k), 0)

    def along_lanes(column):
        return jnp.sum(jnp.where(own, column.astype(F32), 0.0), axis=0, keepdims=True)

    def pick(value, low):
        high = value.astype(BF16).astype(F32)
        return jnp.where(low, value - high, high).astype(BF16)

    part, group = part_group(lax.broadcasted_iota(jnp.int32, (1, k), 1))
    row_freq = along_lanes(freq_x).astype(jnp.int32)
    weight = along_lanes(open_) * (1.0 / math.sqrt(beams))
    x = lax.broadcasted_iota(jnp.int32, (n, k), 0) * row_freq
    for p in range(probes):
        wanted = lax.broadcasted_iota(jnp.int32, position.shape, 0) == place_ref[0] * probes + p
        at = jnp.sum(jnp.where(wanted, position.astype(F32), 0.0), axis=0, keepdims=True).astype(jnp.int32)
        mixing = (freq_x * at[:, 0:1] + freq_y * at[:, 1:2]) & (n - 1)
        turn = -along_lanes(mixing).astype(jnp.int32) - quarter * part
        left_ref[p] = pick(cos_turns(x + turn, n) * weight, group == 1)
    part, group = part_group(lax.broadcasted_iota(jnp.int32, (k, n), 0))
    turn = lax.broadcasted_iota(jnp.int32, (k, n), 1) * jnp.concatenate([freq_y] * 6, axis=0)
    for c, extra in enumerate((quarter * part, quarter * part - quarter)):
        right_ref[c] = pick(cos_turns(turn + extra, n), group == 2)


def probe_waves(grid, beam_index, aperture, position, place):
    probes = position.shape[0] // QUAD
    k = 6 * beam_index.shape[0]
    beam = jnp.concatenate([beam_index, aperture[:, None]], axis=1)
    vmem = pl.BlockSpec(memory_space=pltpu.VMEM)
    return pl.pallas_call(
        wave_kernel,
        name="probe_waves",
        in_specs=[pl.BlockSpec(memory_space=pltpu.SMEM), vmem, vmem],
        out_specs=[vmem, vmem],
        out_shape=[jax.ShapeDtypeStruct((probes, grid, k), BF16), jax.ShapeDtypeStruct((2, k, grid), BF16)],
        compiler_params=pltpu.CompilerParams(vmem_limit_bytes=12 << 20),
    )(place.astype(jnp.int32).reshape(1), position, beam)


def split(x):
    high = x.astype(BF16)
    return high, (x - high.astype(F32)).astype(BF16)


def dot(a, b):
    return jnp.dot(a, b, preferred_element_type=F32)


def dot3(ah, al, bh, bl):
    return dot(ah, bh) + dot(al, bh) + dot(ah, bl)


def butterfly(parts, sign):
    (r0, i0), (r1, i1), (r2, i2), (r3, i3) = parts
    sr, si, dr, di = r0 + r2, i0 + i2, r0 - r2, i0 - i2
    tr, ti, er, ei = r1 + r3, i1 + i3, r1 - r3, i1 - i3
    up = (dr - sign * ei, di + sign * er)
    down = (dr + sign * ei, di - sign * er)
    return [(sr + tr, si + ti), up, (sr - tr, si - ti), down]


def chebyshev(function, top, terms):
    fit = np.polynomial.chebyshev.Chebyshev.interpolate(function, terms - 1, domain=[0.0, top])
    return [float(v) for v in fit.convert(kind=np.polynomial.Polynomial).coef]


COS = chebyshev(lambda t: np.cos(np.sqrt(t)), 2.56, 5)
SIN = chebyshev(lambda t: np.sinc(np.sqrt(t) / np.pi), 2.56, 5)


def horner(coefficients, t):
    value = coefficients[-1]
    for coefficient in coefficients[-2::-1]:
        value = value * t + coefficient
    return value


def cos_sin(v):
    t = v * v
    return horner(COS, t), v * horner(SIN, t)


def transmit_kernel(own_ref, *refs, blocks):
    pieces, (tr_ref, ti_ref) = refs[:-2], refs[-2:]
    block_rows = tr_ref.shape[0] // blocks
    each = blocks // len(pieces)
    for b in range(blocks):
        place = pl.multiple_of((own_ref[0] ^ b) * block_rows, block_rows)
        first = b % each * block_rows
        c, s = cos_sin(pieces[b // each][first : first + block_rows, :].astype(F32))
        tr_ref[pl.ds(place, block_rows), :] = c
        ti_ref[pl.ds(place, block_rows), :] = s


def transmit(own, pieces, blocks):
    vmem = pl.BlockSpec(memory_space=pltpu.VMEM)
    columns = pieces[0].shape[1]
    shape = jax.ShapeDtypeStruct((sum(piece.shape[0] for piece in pieces), columns), F32)
    return pl.pallas_call(
        functools.partial(transmit_kernel, blocks=blocks),
        name="transmit",
        in_specs=[pl.BlockSpec(memory_space=pltpu.SMEM)] + [vmem] * len(pieces),
        out_specs=[vmem, vmem],
        out_shape=[shape, shape],
        compiler_params=pltpu.CompilerParams(vmem_limit_bytes=8 << 20),
    )(own, *pieces)


def clear_padding(uh, ul, kp):
    q = uh.shape[1] // 2
    for spectrum in (uh, ul):
        for c in range(4):
            for first in (0, q):
                spectrum[c, first + kp : first + q] = jnp.zeros((q - kp, spectrum.shape[2]), BF16)


def forward(prepare, wave_ref, tr_ref, ti_ref, wh, wl, vh, vl, pr, pi, scratch, after):
    yh, yl, sr, si, zh, zl, uh, ul = scratch
    n = tr_ref.shape[0]
    q = n // 4
    kp = pr.shape[1]
    rows = 32

    def fold_lanes(first):
        at = pl.ds(first, rows)
        parts = []
        for j in range(4):
            lanes = pl.ds(j * q, q)
            wr, wi = wave_ref[0, at, lanes], wave_ref[1, at, lanes]
            cr, ci = tr_ref[at, lanes], ti_ref[at, lanes]
            parts.append((wr * cr - wi * ci, wr * ci + wi * cr))
        for c, (r, i) in enumerate(butterfly(parts, -1.0)):
            yh[c, at, :q], yl[c, at, :q] = split(r)
            yh[c, at, q:], yl[c, at, q:] = split(i)

    def fold_rows(l):
        lanes = pl.ds(l * q, q)
        for first in range(0, q, rows):
            parts = [(sr[pl.ds(j * q + first, rows), lanes], si[pl.ds(j * q + first, rows), lanes]) for j in range(4)]
            for c, (r, i) in enumerate(butterfly(parts, -1.0)):
                zh[c, pl.ds(first, rows), lanes], zl[c, pl.ds(first, rows), lanes] = split(r)
                zh[c, pl.ds(q + first, rows), lanes], zl[c, pl.ds(q + first, rows), lanes] = split(i)

    step = n // ROW_STEPS
    for b in range(ROW_STEPS):
        at = pl.ds(b * step, step)
        prepare(at)
        for first in range(b * step, (b + 1) * step, rows):
            fold_lanes(first)
        for c in range(4):
            out = dot3(yh[c, at], yl[c, at], wh[c], wl[c])
            sr[at, c * q : (c + 1) * q] = out[:, :q]
            si[at, c * q : (c + 1) * q] = out[:, q:]
            if b == ROW_STEPS - 1:
                fold_rows(c)
    for h in range(2):
        lanes = pl.ds(h * 2 * q, 2 * q)
        for c in range(4):
            zhc, zlc = zh[c, :, lanes], zl[c, :, lanes]
            r = dot3(vh[c, :kp], vl[c, :kp], zhc, zlc)
            i = dot3(vh[c, q : q + kp], vl[c, q : q + kp], zhc, zlc)
            k = 1 if c == 3 else c
            re, im = pr[k, :, lanes], pi[k, :, lanes]
            uh[c, :kp, lanes], ul[c, :kp, lanes] = split(r * re - i * im)
            uh[c, q : q + kp, lanes], ul[c, q : q + kp, lanes] = split(r * im + i * re)
        after(h)


def first_kernel(probe, tr, ti, left_ref, right_ref, wh, wl, vh, vl, pr, pi, out_ref, wave_ref, *scratch):
    def prepare(at):
        for c in range(2):
            wave_ref[c, at] = dot(left_ref[probe, at], right_ref[c])

    slice_kernel(prepare, tr, ti, wave_ref, wh, wl, vh, vl, pr, pi, out_ref, *scratch)


def middle_kernel(tr, ti, wave_ref, wh, wl, vh, vl, pr, pi, out_ref, *scratch):
    slice_kernel(lambda at: None, tr, ti, wave_ref, wh, wl, vh, vl, pr, pi, out_ref, *scratch)


def slice_kernel(prepare, tr, ti, wave_ref, wh, wl, vh, vl, pr, pi, out_ref, yh, yl, sr, si, zh, zl, uh, ul, g, hr):
    n = tr.shape[0]
    q = n // 4
    rows = 32

    clear_padding(uh, ul, pr.shape[1])

    def unfold_rows(l):
        lanes = pl.ds(l * q, q)
        for first in range(0, q, rows):
            parts = [(g[c, pl.ds(first, rows), lanes], g[c, pl.ds(q + first, rows), lanes]) for c in range(4)]
            for j, (r, i) in enumerate(butterfly(parts, 1.0)):
                at = pl.ds(j * q + first, rows)
                yh[l, at, :q], yl[l, at, :q] = split(r)
                yh[l, at, q:], yl[l, at, q:] = split(i)

    def after(h):
        lanes = pl.ds(h * 2 * q, 2 * q)
        for c in range(4):
            g[c, :, lanes] = dot3(wh[c], wl[c], uh[c, :, lanes], ul[c, :, lanes])
        for l in (2 * h, 2 * h + 1):
            unfold_rows(l)

    forward(prepare, wave_ref, tr, ti, wh, wl, vh, vl, pr, pi, (yh, yl, sr, si, zh, zl, uh, ul), after)
    step = n // ROW_STEPS
    for b in range(ROW_STEPS):
        at = pl.ds(b * step, step)
        for c in range(4):
            hr[c, at] = dot3(yh[c, at], yl[c, at], vh[c], vl[c])
        for first in range(b * step, (b + 1) * step, rows):
            at = pl.ds(first, rows)
            parts = [(hr[c, at, :q], hr[c, at, q:]) for c in range(4)]
            for j, (r, i) in enumerate(butterfly(parts, 1.0)):
                out_ref[0, at, pl.ds(j * q, q)] = r
                out_ref[1, at, pl.ds(j * q, q)] = i


def last_kernel(probes, tr, ti, *refs):
    waves, (wh, wl, vh, vl, pr, pi, dh, dl, keep_ref, away_ref) = refs[:probes], refs[probes : probes + 10]
    scratch = refs[probes + 10 :]
    each = len(scratch) // probes
    for p in range(probes):
        own = scratch[p * each : (p + 1) * each]
        last_one(tr, ti, waves[p], wh, wl, vh, vl, pr, pi, dh, dl, keep_ref.at[p], away_ref.at[p], *own)


def last_one(tr, ti, wave_ref, wh, wl, vh, vl, pr, pi, dh, dl, keep_ref, away_ref, yh, yl, sr, si, zh, zl, uh, ul):
    n = tr.shape[0]
    q = n // 4
    take = dh.shape[1] // 2

    clear_padding(uh, ul, pr.shape[1])

    half_out = []

    def after(h):
        lanes = pl.ds(h * 2 * q, 2 * q)
        out = dot3(dh[0], dl[0], uh[0, :, lanes], ul[0, :, lanes])
        for c in range(1, 4):
            out = out + dot3(dh[c], dl[c], uh[c, :, lanes], ul[c, :, lanes])
        half_out.append(out)

    forward(lambda at: None, wave_ref, tr, ti, wh, wl, vh, vl, pr, pi, (yh, yl, sr, si, zh, zl, uh, ul), after)
    parts = []
    for c in range(4):
        lanes = slice(c % 2 * q, c % 2 * q + q)
        out = half_out[c // 2]
        high, low = split(jnp.concatenate([out[:take, lanes], out[take:, lanes]], axis=1))
        back = dot3(high, low, vh[c], vl[c])
        parts.append((back[:, :q], back[:, q:]))
    for j, (r, i) in enumerate(butterfly(parts, 1.0)[1:3]):
        for c, part in enumerate((r, i)):
            keep_ref[c, :, j * q : (j + 1) * q] = part[: take // 2]
            away_ref[c, :, j * q : (j + 1) * q] = part[take // 2 :]


def gather_kernel(place_ref, pair_ref, other_ref, out_ref, buffer):
    rows, _, probes, _ = out_ref.shape
    per_device = probes // QUAD
    for y in range(2):
        for core in range(2):
            slot = (place_ref[0] ^ (2 * y + core)) * per_device
            for p in range(per_device):
                source = other_ref[y * per_device + p] if core else pair_ref[y * per_device + p, :, :rows]
                buffer[slot + p] = source
    for r in range(rows):
        for c in range(2):
            out_ref[r, c] = buffer[:, c, r, :]


def forward_scratch(n):
    q = n // 4
    return [
        pltpu.VMEM((4, n, 2 * q), BF16),
        pltpu.VMEM((4, n, 2 * q), BF16),
        pltpu.VMEM((n, n), F32),
        pltpu.VMEM((n, n), F32),
        pltpu.VMEM((4, 2 * q, n), BF16),
        pltpu.VMEM((4, 2 * q, n), BF16),
        pltpu.VMEM((4, 2 * q, n), BF16),
        pltpu.VMEM((4, 2 * q, n), BF16),
    ]


def run_kernel(kernel, inputs, out_shapes, first, extra):
    n = inputs[0].shape[-1]
    vmem = pl.BlockSpec(memory_space=pltpu.VMEM)
    return pl.pallas_call(
        kernel,
        in_specs=[vmem] * len(inputs),
        out_specs=[vmem] * len(out_shapes),
        out_shape=[jax.ShapeDtypeStruct(shape, F32) for shape in out_shapes],
        scratch_shapes=first + forward_scratch(n) + extra,
        compiler_params=pltpu.CompilerParams(vmem_limit_bytes=36 << 20),
    )(*inputs)


def local(potential_pool, slice_owner, beam_index, aperture, probe_position):
    grid = potential_pool.shape[-1]
    crop = grid // 2
    margin = grid // 4
    q = grid // 4
    groups = lax.axis_size("wide")
    device = lax.axis_index("wide")
    probes = probe_position.shape[0]
    per_device = probes // QUAD
    quad_rows = crop // (groups // QUAD)
    own_rows = crop // groups
    place = device % QUAD
    quad = device // QUAD

    slabs, own = spread_slabs(potential_pool[0], slice_owner, groups, device)
    blocks = groups // 2

    factors = probe_waves(grid, beam_index, aperture, probe_position, place)
    forward_table, inverse_table, prop, last_rows = make_tables(grid, margin + quad * quad_rows, place * own_rows, quad_rows)
    tables = (*forward_table, *inverse_table, *prop)
    extra = [pltpu.VMEM((4, 2 * q, grid), F32), pltpu.VMEM((4, grid, 2 * q), F32)]
    wave = [pltpu.VMEM((2, grid, grid), F32)]
    turned = transmit(own, slabs[0], blocks)
    waves = [
        run_kernel(functools.partial(first_kernel, p), (*turned, *factors, *tables), [(2, grid, grid)], wave, extra)[0]
        for p in range(per_device)
    ]
    for slab in slabs[1:-1]:
        turned = transmit(own, slab, blocks)
        waves = [run_kernel(middle_kernel, (*turned, w, *tables), [w.shape], [], extra)[0] for w in waves]
    turned = transmit(own, slabs[-1], blocks)

    inputs = (*turned, *waves, *tables, *last_rows)
    shape = (per_device, 2, quad_rows // 2, crop)
    more = forward_scratch(grid) * (per_device - 1)
    keep, away = run_kernel(functools.partial(last_kernel, per_device), inputs, [shape, shape], [], more)
    pair = jnp.concatenate([keep, flip(away, 2, groups)], axis=0)
    other = flip(pair[:, :, own_rows:], 1, groups)
    vmem = pl.BlockSpec(memory_space=pltpu.VMEM)
    return pl.pallas_call(
        gather_kernel,
        name="gather_probes",
        in_specs=[pl.BlockSpec(memory_space=pltpu.SMEM), vmem, vmem],
        out_specs=vmem,
        out_shape=jax.ShapeDtypeStruct((own_rows, 2, probes, crop), F32),
        scratch_shapes=[pltpu.VMEM((probes, 2, own_rows, crop), F32)],
        compiler_params=pltpu.CompilerParams(vmem_limit_bytes=8 << 20),
    )(place.astype(jnp.int32).reshape(1), pair, other)


def solution(mesh):
    placed = (P(("parts", "wide"), None, None), P("parts"), P(), P(), P("parts", None))

    return jax.shard_map(
        local,
        mesh=mesh,
        in_specs=placed,
        out_specs=P(("parts", "wide"), None, None, None),
        check_vma=False,
    )
```
